512 devices in a mesh: ctx: 64 (over x, z_lo, y), tp: 8 (over z_hi, core).
Axes of the slice: x: 4, y: 4, z: 16 (z_hi: 4, z_lo: 4; z = z_hi * 4 + z_lo), core: 2. Of those that a mesh axis runs over, the one named last changes fastest.
Arguments:
- layer_cotangent: bfloat16 [16384, 5376], P('ctx', 'tp'), may hold values from -6 to 6
- out_weight: bfloat16 [2048, 5376], P(None, 'tp'), may hold values from -0.078125 to 0.078125
- queries: bfloat16 [16384, 2048], P('ctx', 'tp'), may hold values from -38 to 38
- keys: bfloat16 [16384, 1024], P('ctx', 'tp'), may hold values from -13 to 13
- values: bfloat16 [16384, 1024], P('ctx', 'tp'), may hold values from -6 to 6
Outputs:
- query_grads: bfloat16 [16384, 2048], P('ctx', 'tp')
- key_gradients: bfloat16 [16384, 1024], P('ctx', 'tp')
- value_gradients: bfloat16 [16384, 1024], P('ctx', 'tp')
The draws below stay inside these ranges and needn't reach their ends.
All inputs are finite; a program needn't handle non-finite values.
Results may differ from the reference program's by a relative error of at most 0.03.
Values may be sent and summed in bfloat16 or wider, within the bound.
A program may use at most 64 MiB of HBM per device.

```python
import jax
import jax.numpy as jnp
from jax import lax

D = 5376
QUERY_HEAD_COUNT = 16
KEY_VALUE_HEADS = 8
HEAD_SIZE = 128
WINDOW_LENGTH = 1024
T_DEV = 256
TOKEN_COUNT = 16384
N_TP = 8


def shared_fields(key):
    key_row_block = jax.random.normal(jax.random.fold_in(key, 11), (TOKEN_COUNT, KEY_VALUE_HEADS, HEAD_SIZE), jnp.float32)
    key_row_block = jnp.clip(key_row_block, -4.0, 4.0)
    key_scale = jnp.exp(jax.random.uniform(jax.random.fold_in(key, 12), (TOKEN_COUNT, 1, 1), jnp.float32, -1.15, 1.15))
    key_row_block = key_row_block * key_scale
    query_rows = jax.random.normal(jax.random.fold_in(key, 13), (TOKEN_COUNT, QUERY_HEAD_COUNT, HEAD_SIZE), jnp.float32)
    query_rows = jnp.clip(query_rows, -4.0, 4.0)
    query_scale = jnp.exp(jax.random.uniform(jax.random.fold_in(key, 14), (TOKEN_COUNT, 1, 1), jnp.float32, -1.15, 1.15))
    query_rows = query_rows * query_scale
    return (query_rows, key_row_block)


def draw_queries(key, part):
    query_rows, key_row_block = shared_fields(key)
    return query_rows.reshape(TOKEN_COUNT, QUERY_HEAD_COUNT * HEAD_SIZE).astype(jnp.bfloat16)


def draw_keys(key, part):
    query_rows, key_row_block = shared_fields(key)
    return key_row_block.reshape(TOKEN_COUNT, KEY_VALUE_HEADS * HEAD_SIZE).astype(jnp.bfloat16)


def block_levels(own_key, dims, pieces, low, largest):
    gain, own = 1.0, jax.random.fold_in(own_key, 6)
    for dim, blocks in pieces:
        draws = jnp.exp(jax.random.uniform(jax.random.fold_in(own, dim), (blocks,), jnp.float32, low / len(pieces), largest / len(pieces)))
        gain = gain * jnp.repeat(draws, dims[dim] // blocks).reshape([-1 if axis == dim else 1 for axis in range(len(dims))])
    return gain


def bell_draw(key, shape, width, bound, split=(), kind=jnp.bfloat16):
    loudness = block_levels(key, shape, split, -0.22, 0.18) if split else 1.0
    values = jax.random.normal(key, shape, jnp.float32) * width * loudness
    return jnp.minimum(jnp.maximum(values, -bound), bound).astype(kind)


def setup_inputs(seed: int = 0) -> dict:
    splits = jax.random.split(jax.random.key(seed), 6)
    return {
        "layer_cotangent": bell_draw(splits[0], (TOKEN_COUNT, D), 1.0, 6.0, ((0, 64), (1, 8))),
        "out_weight": bell_draw(splits[1], (QUERY_HEAD_COUNT * HEAD_SIZE, D), D ** -0.5, 0.078125, ((1, 8),)),
        "queries": draw_queries(jax.random.fold_in(splits[5], 71), 0),
        "keys": draw_keys(jax.random.fold_in(splits[5], 71), 0),
        "values": bell_draw(splits[4], (TOKEN_COUNT, KEY_VALUE_HEADS * HEAD_SIZE), 1.0, 6.0, ((0, 64), (1, 8))),
    }


score_scale = 168.0 ** -0.5


def rounded(term):
    return lax.optimization_barrier(term.astype(jnp.bfloat16)).astype(jnp.float32)


def reference(layer_cotangent, out_weight, queries, keys, values):
    parts = D // N_TP
    query_group = QUERY_HEAD_COUNT // KEY_VALUE_HEADS
    cot_parts = layer_cotangent.reshape(TOKEN_COUNT, N_TP, parts).transpose(1, 0, 2)
    weight_parts = out_weight.reshape(QUERY_HEAD_COUNT * HEAD_SIZE, N_TP, parts).transpose(1, 0, 2)

    def add_part(total, pair):
        term = lax.dot_general(pair[0], pair[1], (((1,), (1,)), ((), ())), preferred_element_type=jnp.float32)
        term = lax.optimization_barrier(term.astype(jnp.bfloat16))
        return total + term.astype(jnp.float32), None

    head_total, unused = lax.scan(add_part, jnp.zeros((TOKEN_COUNT, QUERY_HEAD_COUNT * HEAD_SIZE), jnp.float32), (cot_parts, weight_parts))
    head_gradients = head_total.astype(jnp.bfloat16)

    block = T_DEV
    nblocks = TOKEN_COUNT // block
    query_quad = queries.reshape(TOKEN_COUNT, KEY_VALUE_HEADS, query_group, HEAD_SIZE)
    gradient_quad = head_gradients.reshape(TOKEN_COUNT, KEY_VALUE_HEADS, query_group, HEAD_SIZE)
    padding_rows = jnp.zeros((WINDOW_LENGTH, KEY_VALUE_HEADS, HEAD_SIZE), jnp.bfloat16)
    key_padding = jnp.concatenate([padding_rows, keys.reshape(TOKEN_COUNT, KEY_VALUE_HEADS, HEAD_SIZE)], axis=0)
    value_padding = jnp.concatenate([padding_rows, values.reshape(TOKEN_COUNT, KEY_VALUE_HEADS, HEAD_SIZE)], axis=0)

    def one_block(carry, index):
        key_total, value_total = carry
        start = (index * block).astype(jnp.int32)
        query_blk = lax.dynamic_slice_in_dim(query_quad, start, block, 0).astype(jnp.float32)
        grad_blk = lax.dynamic_slice_in_dim(gradient_quad, start, block, 0).astype(jnp.float32)
        key_blk = lax.dynamic_slice_in_dim(key_padding, start, block + WINDOW_LENGTH, 0).astype(jnp.float32)
        value_blk = lax.dynamic_slice_in_dim(value_padding, start, block + WINDOW_LENGTH, 0).astype(jnp.float32)
        query_pos = start + jnp.arange(block, dtype=jnp.int32)
        key_pos = start - WINDOW_LENGTH + jnp.arange(block + WINDOW_LENGTH, dtype=jnp.int32)
        apart = query_pos[:, None] - key_pos[None, :]
        visible = (apart >= 0) & (apart <= WINDOW_LENGTH - 1) & (key_pos[None, :] >= 0)
        scores = jnp.einsum('qhgd,khd->hgqk', query_blk, key_blk) * score_scale
        scores = jnp.where(visible, scores, -jnp.inf)
        top = jnp.max(scores, axis=-1, keepdims=True)
        expo = jnp.exp(scores - top)
        probs = expo / jnp.sum(expo, axis=-1, keepdims=True)
        probs_low = probs.astype(jnp.bfloat16)
        dprobs = jnp.einsum('qhgd,khd->hgqk', grad_blk, value_blk)
        delta = jnp.sum(probs * dprobs, axis=-1, keepdims=True)
        dscores = (probs * (dprobs - delta) * score_scale).astype(jnp.bfloat16)
        query_part = jnp.einsum('hgqk,khd->qhgd', dscores.astype(jnp.float32), key_blk)
        key_part = jnp.einsum('hgqk,qhgd->khd', dscores.astype(jnp.float32), query_blk)
        value_part = jnp.einsum('hgqk,qhgd->khd', probs_low.astype(jnp.float32), grad_blk)
        key_part = jnp.concatenate([rounded(key_part[:WINDOW_LENGTH]), key_part[WINDOW_LENGTH:]], axis=0)
        value_part = jnp.concatenate([rounded(value_part[:WINDOW_LENGTH]), value_part[WINDOW_LENGTH:]], axis=0)
        key_total = lax.dynamic_update_slice_in_dim(key_total, lax.dynamic_slice_in_dim(key_total, start, block + WINDOW_LENGTH, 0) + key_part, start, 0)
        value_total = lax.dynamic_update_slice_in_dim(value_total, lax.dynamic_slice_in_dim(value_total, start, block + WINDOW_LENGTH, 0) + value_part, start, 0)
        return (key_total, value_total), query_part.astype(jnp.bfloat16)

    zero_padding = jnp.zeros((TOKEN_COUNT + WINDOW_LENGTH, KEY_VALUE_HEADS, HEAD_SIZE), jnp.float32)
    running_totals, query_blocks = lax.scan(one_block, (zero_padding, zero_padding), jnp.arange(nblocks, dtype=jnp.int32))
    query_grads = query_blocks.reshape(TOKEN_COUNT, QUERY_HEAD_COUNT * HEAD_SIZE)
    key_gradients = running_totals[0][WINDOW_LENGTH:].reshape(TOKEN_COUNT, KEY_VALUE_HEADS * HEAD_SIZE).astype(jnp.bfloat16)
    value_gradients = running_totals[1][WINDOW_LENGTH:].reshape(TOKEN_COUNT, KEY_VALUE_HEADS * HEAD_SIZE).astype(jnp.bfloat16)
    return (query_grads, key_gradients, value_gradients)
```

```python
import jax
import jax.numpy as jnp
from jax import lax
from jax.experimental import pallas as pl
from jax.experimental.pallas import tpu as pltpu
from jax.sharding import PartitionSpec as P

HEAD_SIZE = 128
Y = 4
score_scale = 168.0 ** (-0.5)
MESH = pl.DeviceIdType.MESH
F32 = jnp.float32
BF16 = jnp.bfloat16


def dot(a, b, ca, cb):
    return lax.dot_general(a, b, (((ca,), (cb,)), ((), ())), preferred_element_type=F32)


def make_kernel(n_ctx, n_tp, t):
    n_u = n_tp // 2
    back = 4
    h = HEAD_SIZE
    order = (2, 1, 3, 0)

    def kernel(
        cot_hbm, w_hbm, q_hbm, k_hbm, v_hbm,
        dq_ref, dk_ref, dv_ref,
        cot, w, q_in, q2, kv, kt,
        pair_send, pair_recv, own_part, ring_send, s1_recv, d_recv, c_recv, grads,
        probs, probs_low, dprobs, dscores,
        g_send, g_recv, z_send, z_recv, g_own,
        load_sem, kvz_sem, kvy_sem, pair_sem, s1_sem, d_sem, c_sem, gk_sem, gv_sem, z_sem,
    ):
        c = lax.axis_index("ctx")
        tp = lax.axis_index("tp")
        u = tp // 2
        a = tp % 2
        y = c % Y
        plane = c - y

        loads = [
            pltpu.make_async_copy(k_hbm, kv.at[back, 0], load_sem.at[0]),
            pltpu.make_async_copy(v_hbm, kv.at[back, 1], load_sem.at[1]),
            pltpu.make_async_copy(cot_hbm, cot, load_sem.at[2]),
            pltpu.make_async_copy(w_hbm, w, load_sem.at[3]),
            pltpu.make_async_copy(q_hbm, q_in, load_sem.at[4]),
        ]
        for load in loads:
            load.start()

        following = ((c + back) % n_ctx, tp)
        preceding = ((c + n_ctx - back) % n_ctx, tp)
        other_core = (c, u * 2 + (1 - a))
        up = (c, (tp + 2) % n_tp)
        down = (c, (tp + n_tp - 2) % n_tp)

        def along(r):
            return (plane + (y + r) % Y, tp)

        barrier = pltpu.get_barrier_semaphore()
        partners = [following, preceding, other_core, up, down, along(1), along(2), along(3)]
        for partner in partners:
            pl.semaphore_signal(barrier, inc=1, device_id=partner, device_id_type=MESH)

        def remote(src, dst, sems, index, device):
            return pltpu.make_async_remote_copy(
                src_ref=src, dst_ref=dst, send_sem=sems.at[0, index], recv_sem=sems.at[1, index],
                device_id=device, device_id_type=MESH,
            )

        loads[0].wait()
        loads[1].wait()
        pl.semaphore_wait(barrier, len(partners))

        kvz = remote(kv.at[back], kv.at[0], kvz_sem, 0, following)
        kvz.start()

        loads[2].wait()
        loads[3].wait()

        def part(du, core):
            dest = ((u + du) % n_u) * 2 + core
            rows = w[pl.ds(pl.multiple_of(dest * 2 * h, 2 * h), 2 * h), :]
            return dot(cot[...], rows, 1, 1)

        pairs = []
        for i, du in enumerate(order):
            term = part(du, 1 - a)
            pair_send[i, 0:t] = term[:, :h].astype(BF16)
            pair_send[i, t:] = term[:, h:].astype(BF16)
            copy = remote(pair_send.at[i], pair_recv.at[i], pair_sem, i, other_core)
            copy.start()
            pairs.append(copy)

        s1 = [
            remote(ring_send.at[0, 0], s1_recv.at[0], s1_sem, 0, up),
            remote(ring_send.at[0, 1], s1_recv.at[1], s1_sem, 1, down),
        ]
        direct = [
            remote(ring_send.at[1, 1], d_recv.at[0], d_sem, 0, up),
            remote(ring_send.at[2, 0], d_recv.at[1], d_sem, 1, down),
        ]
        combined = [
            remote(ring_send.at[1, 0], c_recv.at[0], c_sem, 0, up),
            remote(ring_send.at[2, 1], c_recv.at[1], c_sem, 1, down),
        ]
        for i, du in enumerate(order):
            term = part(du, a)
            pairs[i].wait_recv()
            low = term[:, :h] + pair_recv[i, 0:t].astype(F32)
            high = term[:, h:] + pair_recv[i, t:].astype(F32)
            if i == 0:
                ring_send[0, 0] = low.astype(BF16)
                ring_send[0, 1] = high.astype(BF16)
                s1[0].start()
                s1[1].start()
            elif i == 1:
                ring_send[1, 1] = high.astype(BF16)
                direct[0].start()
                own_part[0] = low
            elif i == 2:
                ring_send[2, 0] = low.astype(BF16)
                direct[1].start()
                own_part[1] = high
            else:
                own_part[2] = low
                own_part[3] = high

        kvz.wait_recv()
        kvy = []
        for r in (2, 1, 3):
            source = jnp.where(y < r, back, 0)
            copy = remote(kv.at[source], kv.at[r], kvy_sem, r - 1, along(Y - r))
            copy.start()
            kvy.append(copy)

        s1[0].wait_recv()
        ring_send[1, 0] = (own_part[0] + s1_recv[0].astype(F32)).astype(BF16)
        combined[0].start()
        s1[1].wait_recv()
        ring_send[2, 1] = (own_part[1] + s1_recv[1].astype(F32)).astype(BF16)
        combined[1].start()

        loads[4].wait()
        q2[0:t] = q_in[:, :h]
        q2[t:] = q_in[:, h:]

        key_row = lax.broadcasted_iota(jnp.int32, (t, 2 * t), 0)
        query_col = lax.broadcasted_iota(jnp.int32, (t, 2 * t), 1) % t
        top = jnp.full((1, 2 * t), -jnp.inf, F32)
        for slot in (4, 0, 2, 1, 3):
            if slot in (1, 2, 3):
                kvy[(2, 1, 3).index(slot)].wait_recv()
            scores = dot(kv[slot, 0], q2[...], 1, 1) * score_scale
            here = c + slot >= back
            if slot == back:
                scores = jnp.where(key_row <= query_col, scores, -jnp.inf)
            elif slot == 0:
                scores = jnp.where((key_row > query_col) & here, scores, -jnp.inf)
            else:
                scores = jnp.where(here, scores, -jnp.inf)
            probs[slot] = scores
            top = jnp.maximum(top, jnp.max(scores, axis=0, keepdims=True))
            kt[slot] = kv[slot, 0].T
        total = jnp.zeros((1, 2 * t), F32)
        for slot in range(back + 1):
            expo = jnp.exp(probs[slot] - top)
            probs[slot] = expo
            total = total + jnp.sum(expo, axis=0, keepdims=True)
        inverse = 1.0 / total
        for slot in range(back + 1):
            prob = probs[slot] * inverse
            probs[slot] = prob
            probs_low[slot] = prob.astype(BF16)

        direct[0].wait_recv()
        direct[1].wait_recv()
        combined[0].wait_recv()
        combined[1].wait_recv()
        grads[0:t] = (
            own_part[2] + d_recv[1].astype(F32) + c_recv[0].astype(F32)
        ).astype(BF16)
        grads[t:] = (
            own_part[3] + d_recv[0].astype(F32) + c_recv[1].astype(F32)
        ).astype(BF16)

        gk, gv = {}, {}
        for r in (2, 1, 3):
            gv[r] = remote(g_send.at[r - 1, 1], g_recv.at[r - 1, 1], gv_sem, r - 1, along(r))
            gk[r] = remote(g_send.at[r - 1, 0], g_recv.at[r - 1, 0], gk_sem, r - 1, along(r))
            g_send[r - 1, 1] = dot(probs_low[r], grads[...], 1, 0).astype(BF16)
            gv[r].start()
        delta = jnp.zeros((1, 2 * t), F32)
        for slot in range(back + 1):
            dp = dot(kv[slot, 1], grads[...], 1, 1)
            dprobs[slot] = dp
            delta = delta + jnp.sum(probs[slot] * dp, axis=0, keepdims=True)
        for slot in (2, 1, 3, 0, 4):
            ds = (probs[slot] * (dprobs[slot] - delta) * score_scale).astype(BF16)
            dscores[slot] = ds
            key_part = dot(ds, q2[...], 1, 0)
            if slot in (1, 2, 3):
                g_send[slot - 1, 0] = key_part.astype(BF16)
                gk[slot].start()
            else:
                g_own[slot // 4, 0] = key_part
                g_own[slot // 4, 1] = dot(probs_low[slot], grads[...], 1, 0)
        turned = jnp.zeros((h, 2 * t), F32)
        for slot in range(back + 1):
            turned = turned + dot(kt[slot], dscores[slot], 1, 0)
        dq_ref[:, :h] = turned[:, :t].T.astype(BF16)
        dq_ref[:, h:] = turned[:, t:].T.astype(BF16)

        for part_index, copies in ((1, gv), (0, gk)):
            for r in (2, 1, 3):
                copies[r].wait_recv()
                arrived = g_recv[r - 1, part_index].astype(F32)
                earlier = y >= r
                g_own[0, part_index] += jnp.where(earlier, arrived, 0.0)
                g_own[1, part_index] += jnp.where(earlier, 0.0, arrived)
        z_send[...] = g_own[0].astype(BF16)
        last = remote(z_send, z_recv, z_sem, 0, preceding)
        last.start()
        last.wait_recv()
        dk_ref[...] = (g_own[1, 0] + z_recv[0].astype(F32)).astype(BF16)
        dv_ref[...] = (g_own[1, 1] + z_recv[1].astype(F32)).astype(BF16)

        for copy in [kvz, *kvy, *pairs, *s1, *direct, *combined, *gk.values(), *gv.values(), last]:
            copy.wait_send()

    return kernel


def solution(mesh):
    n_ctx, n_tp = mesh.shape["ctx"], mesh.shape["tp"]

    def local(layer_cotangent, out_weight, queries, keys, values):
        t, d = layer_cotangent.shape
        h = HEAD_SIZE
        vmem = pltpu.VMEM
        dma = pltpu.SemaphoreType.DMA
        scratch = [
            vmem((t, d), BF16),
            vmem(out_weight.shape, BF16),
            vmem((t, 2 * h), BF16),
            vmem((2 * t, h), BF16),
            vmem((5, 2, t, h), BF16),
            vmem((5, h, t), BF16),
            vmem((4, 2 * t, h), BF16),
            vmem((4, 2 * t, h), BF16),
            vmem((4, t, h), F32),
            vmem((3, 2, t, h), BF16),
            vmem((2, t, h), BF16),
            vmem((2, t, h), BF16),
            vmem((2, t, h), BF16),
            vmem((2 * t, h), BF16),
            vmem((5, t, 2 * t), F32),
            vmem((5, t, 2 * t), BF16),
            vmem((5, t, 2 * t), F32),
            vmem((5, t, 2 * t), BF16),
            vmem((3, 2, t, h), BF16),
            vmem((3, 2, t, h), BF16),
            vmem((2, t, h), BF16),
            vmem((2, t, h), BF16),
            vmem((2, 2, t, h), F32),
            dma((5,)),
            dma((2, 1)),
            dma((2, 3)),
            dma((2, 4)),
            dma((2, 2)),
            dma((2, 2)),
            dma((2, 2)),
            dma((2, 3)),
            dma((2, 3)),
            dma((2, 1)),
        ]
        return pl.pallas_call(
            make_kernel(n_ctx, n_tp, t),
            out_shape=(
                jax.ShapeDtypeStruct(queries.shape, BF16),
                jax.ShapeDtypeStruct(keys.shape, BF16),
                jax.ShapeDtypeStruct(values.shape, BF16),
            ),
            in_specs=[pl.BlockSpec(memory_space=pl.ANY)] * 5,
            out_specs=tuple(pl.BlockSpec(memory_space=pltpu.VMEM) for _ in range(3)),
            scratch_shapes=scratch,
            compiler_params=pltpu.CompilerParams(
                collective_id=0, has_side_effects=True, vmem_limit_bytes=48 << 20
            ),
            name="attention_backward",
        )(layer_cotangent, out_weight, queries, keys, values)

    in_specs = (P("ctx", "tp"), P(None, "tp"), P("ctx", "tp"), P("ctx", "tp"), P("ctx", "tp"))
    out_specs = (P("ctx", "tp"), P("ctx", "tp"), P("ctx", "tp"))
    return jax.shard_map(local, mesh=mesh, in_specs=in_specs, out_specs=out_specs, check_vma=False)
```

```python
import jax
import jax.numpy as jnp
from jax import lax
from jax.experimental import pallas as pl
from jax.experimental.pallas import tpu as pltpu
from jax.sharding import PartitionSpec as P

HEAD_SIZE = 128
Y = 4
score_scale = 168.0 ** (-0.5)
MESH = pl.DeviceIdType.MESH
F32 = jnp.float32
BF16 = jnp.bfloat16


def dot(a, b, ca, cb):
    return lax.dot_general(a, b, (((ca,), (cb,)), ((), ())), preferred_element_type=F32)


def write_out(dq_in, dk_in, dv_in, dq_out, dk_out, dv_out, sem):
    pairs = ((dq_in, dq_out), (dk_in, dk_out), (dv_in, dv_out))
    copies = [pltpu.make_async_copy(a, b, sem.at[i]) for i, (a, b) in enumerate(pairs)]
    for copy in copies:
        copy.start()
    for copy in copies:
        copy.wait()


def make_kernel(n_ctx, n_tp, t):
    n_u = n_tp // 2
    back = 4
    h = HEAD_SIZE
    order = (2, 1, 3, 0)

    def kernel(
        cot_hbm, w_hbm, q_hbm, k_hbm, v_hbm,
        dq_ref, dk_ref, dv_ref,
        cot_turned, cot, w, q_in, q2, kv, kt,
        pair_send, pair_recv, own_terms, own_part, ring_send, s1_recv, d_recv, c_recv, grads,
        probs, probs_low, dprobs, dscores,
        g_send, g_recv, z_send, z_recv, g_own,
        load_sem, kvz_sem, kvy_sem, pair_sem, s1_sem, d_sem, c_sem, gk_sem, gv_sem, z_sem,
    ):
        c = lax.axis_index("ctx")
        tp = lax.axis_index("tp")
        u = tp // 2
        a = tp % 2
        y = c % Y
        plane = c - y

        loads = [
            pltpu.make_async_copy(k_hbm, kv.at[back, 0], load_sem.at[0]),
            pltpu.make_async_copy(v_hbm, kv.at[back, 1], load_sem.at[1]),
            pltpu.make_async_copy(cot_hbm, cot_turned, load_sem.at[2]),
            pltpu.make_async_copy(w_hbm, w, load_sem.at[3]),
            pltpu.make_async_copy(q_hbm, q_in, load_sem.at[4]),
        ]
        for load in loads:
            load.start()

        following = ((c + back) % n_ctx, tp)
        preceding = ((c + n_ctx - back) % n_ctx, tp)
        other_core = (c, u * 2 + (1 - a))
        up = (c, (tp + 2) % n_tp)
        down = (c, (tp + n_tp - 2) % n_tp)

        def along(r):
            return (plane + (y + r) % Y, tp)

        barrier = pltpu.get_barrier_semaphore()
        partners = [following, preceding, other_core, up, down, along(1), along(2), along(3)]
        for partner in partners:
            pl.semaphore_signal(barrier, inc=1, device_id=partner, device_id_type=MESH)

        def remote(src, dst, sems, index, device):
            return pltpu.make_async_remote_copy(
                src_ref=src, dst_ref=dst, send_sem=sems.at[0, index], recv_sem=sems.at[1, index],
                device_id=device, device_id_type=MESH,
            )

        loads[0].wait()
        loads[1].wait()
        pl.semaphore_wait(barrier, len(partners))

        kvz = remote(kv.at[back], kv.at[0], kvz_sem, 0, following)
        kvz.start()

        loads[2].wait()
        cot[...] = cot_turned[...].T
        loads[3].wait()

        def part(du, core):
            dest = ((u + du) % n_u) * 2 + core
            columns = w[:, pl.ds(pl.multiple_of(dest * 2 * h, 2 * h), 2 * h)]
            return dot(cot[...], columns, 1, 0)

        pairs = []

        def for_other(i):
            term = part(order[i], 1 - a)
            pair_send[i, 0:t] = term[:, :h].astype(BF16)
            pair_send[i, t:] = term[:, h:].astype(BF16)
            copy = remote(pair_send.at[i], pair_recv.at[i], pair_sem, i, other_core)
            copy.start()
            pairs.append(copy)

        def for_this(i):
            own_terms[i] = part(order[i], a)

        def pair_sum(i):
            pairs[i].wait_recv()
            low = own_terms[i, :, :h] + pair_recv[i, 0:t].astype(F32)
            high = own_terms[i, :, h:] + pair_recv[i, t:].astype(F32)
            return low, high

        s1 = [
            remote(ring_send.at[0, 0], s1_recv.at[0], s1_sem, 0, up),
            remote(ring_send.at[0, 1], s1_recv.at[1], s1_sem, 1, down),
        ]
        direct = [
            remote(ring_send.at[1, 1], d_recv.at[0], d_sem, 0, up),
            remote(ring_send.at[2, 0], d_recv.at[1], d_sem, 1, down),
        ]
        combined = [
            remote(ring_send.at[1, 0], c_recv.at[0], c_sem, 0, up),
            remote(ring_send.at[2, 1], c_recv.at[1], c_sem, 1, down),
        ]
        for_other(0)
        for_this(0)
        for_other(1)
        for_other(2)
        low, high = pair_sum(0)
        ring_send[0, 0] = low.astype(BF16)
        ring_send[0, 1] = high.astype(BF16)
        s1[0].start()
        s1[1].start()
        for_other(3)
        for_this(1)
        for_this(2)
        for_this(3)
        low, high = pair_sum(1)
        ring_send[1, 1] = high.astype(BF16)
        own_part[0] = low
        low, high = pair_sum(2)
        ring_send[2, 0] = low.astype(BF16)
        own_part[1] = high
        low, high = pair_sum(3)
        own_part[2] = low
        own_part[3] = high

        kvz.wait_recv()
        kvy = []
        for r in (2, 1, 3):
            source = jnp.where(y < r, back, 0)
            copy = remote(kv.at[source], kv.at[r], kvy_sem, r - 1, along(Y - r))
            copy.start()
            kvy.append(copy)

        s1[0].wait_send()
        direct[0].start()
        s1[1].wait_send()
        direct[1].start()
        s1[0].wait_recv()
        ring_send[1, 0] = (own_part[0] + s1_recv[0].astype(F32)).astype(BF16)
        combined[0].start()
        s1[1].wait_recv()
        ring_send[2, 1] = (own_part[1] + s1_recv[1].astype(F32)).astype(BF16)
        combined[1].start()

        loads[4].wait()
        q2[0:t] = q_in[:, :h]
        q2[t:] = q_in[:, h:]

        key_row = lax.broadcasted_iota(jnp.int32, (t, 2 * t), 0)
        query_col = lax.broadcasted_iota(jnp.int32, (t, 2 * t), 1) % t
        top = jnp.full((1, 2 * t), -jnp.inf, F32)
        for slot in (4, 0, 2, 1, 3):
            if slot in (1, 2, 3):
                kvy[(2, 1, 3).index(slot)].wait_recv()
            scores = dot(kv[slot, 0], q2[...], 1, 1) * score_scale
            here = c + slot >= back
            if slot == back:
                scores = jnp.where(key_row <= query_col, scores, -jnp.inf)
            elif slot == 0:
                scores = jnp.where((key_row > query_col) & here, scores, -jnp.inf)
            else:
                scores = jnp.where(here, scores, -jnp.inf)
            probs[slot] = scores
            top = jnp.maximum(top, jnp.max(scores, axis=0, keepdims=True))
            kt[slot] = kv[slot, 0].T
        total = jnp.zeros((1, 2 * t), F32)
        for slot in range(back + 1):
            expo = jnp.exp(probs[slot] - top)
            probs[slot] = expo
            total = total + jnp.sum(expo, axis=0, keepdims=True)
        inverse = 1.0 / total
        for slot in range(back + 1):
            prob = probs[slot] * inverse
            probs[slot] = prob
            probs_low[slot] = prob.astype(BF16)

        direct[0].wait_recv()
        direct[1].wait_recv()
        combined[0].wait_recv()
        combined[1].wait_recv()
        grads[0:t] = (
            own_part[2] + d_recv[1].astype(F32) + c_recv[0].astype(F32)
        ).astype(BF16)
        grads[t:] = (
            own_part[3] + d_recv[0].astype(F32) + c_recv[1].astype(F32)
        ).astype(BF16)

        gk, gv = {}, {}
        for r in (2, 1, 3):
            gv[r] = remote(g_send.at[r - 1, 1], g_recv.at[r - 1, 1], gv_sem, r - 1, along(r))
            gk[r] = remote(g_send.at[r - 1, 0], g_recv.at[r - 1, 0], gk_sem, r - 1, along(r))
            g_send[r - 1, 1] = dot(probs_low[r], grads[...], 1, 0).astype(BF16)
            gv[r].start()
        delta = jnp.zeros((1, 2 * t), F32)
        for slot in range(back + 1):
            dp = dot(kv[slot, 1], grads[...], 1, 1)
            dprobs[slot] = dp
            delta = delta + jnp.sum(probs[slot] * dp, axis=0, keepdims=True)
        for slot in (2, 1, 3):
            ds = (probs[slot] * (dprobs[slot] - delta) * score_scale).astype(BF16)
            dscores[slot] = ds
            g_send[slot - 1, 0] = dot(ds, q2[...], 1, 0).astype(BF16)
            gk[slot].start()
        for slot in (0, 4):
            g_own[slot // 4, 1] = dot(probs_low[slot], grads[...], 1, 0)
        for slot in (0, 4):
            ds = (probs[slot] * (dprobs[slot] - delta) * score_scale).astype(BF16)
            dscores[slot] = ds
            g_own[slot // 4, 0] = dot(ds, q2[...], 1, 0)

        z_copies = [
            remote(z_send.at[i], z_recv.at[i], z_sem, i, preceding) for i in range(2)
        ]

        def gather(i, copies):
            for r in (1, 3, 2):
                copies[r].wait_recv()
                arrived = g_recv[r - 1, i].astype(F32)
                earlier = y >= r
                g_own[0, i] += jnp.where(earlier, arrived, 0.0)
                g_own[1, i] += jnp.where(earlier, 0.0, arrived)
            z_send[i] = g_own[0, i].astype(BF16)
            z_copies[i].start()

        gather(1, gv)
        turned = jnp.zeros((h, 2 * t), F32)
        for slot in range(back + 1):
            turned = turned + dot(kt[slot], dscores[slot], 1, 0)
        dq_ref[:, :h] = turned[:, :t].T.astype(BF16)
        dq_ref[:, h:] = turned[:, t:].T.astype(BF16)
        gather(0, gk)
        z_copies[1].wait_recv()
        dv_ref[...] = (g_own[1, 1] + z_recv[1].astype(F32)).astype(BF16)
        z_copies[0].wait_recv()
        dk_ref[...] = (g_own[1, 0] + z_recv[0].astype(F32)).astype(BF16)

        for copy in [kvz, *kvy, *pairs, *direct, *combined, *gk.values(), *gv.values(), *z_copies]:
            copy.wait_send()

    return kernel


def solution(mesh):
    n_ctx, n_tp = mesh.shape["ctx"], mesh.shape["tp"]

    def local(layer_cotangent, out_weight, queries, keys, values):
        t, d = layer_cotangent.shape
        h = HEAD_SIZE
        vmem = pltpu.VMEM
        dma = pltpu.SemaphoreType.DMA
        scratch = [
            vmem((d, t), BF16),
            vmem((t, d), BF16),
            vmem(out_weight.shape[::-1], BF16),
            vmem((t, 2 * h), BF16),
            vmem((2 * t, h), BF16),
            vmem((5, 2, t, h), BF16),
            vmem((5, h, t), BF16),
            vmem((4, 2 * t, h), BF16),
            vmem((4, 2 * t, h), BF16),
            vmem((4, t, 2 * h), F32),
            vmem((4, t, h), F32),
            vmem((3, 2, t, h), BF16),
            vmem((2, t, h), BF16),
            vmem((2, t, h), BF16),
            vmem((2, t, h), BF16),
            vmem((2 * t, h), BF16),
            vmem((5, t, 2 * t), F32),
            vmem((5, t, 2 * t), BF16),
            vmem((5, t, 2 * t), F32),
            vmem((5, t, 2 * t), BF16),
            vmem((3, 2, t, h), BF16),
            vmem((3, 2, t, h), BF16),
            vmem((2, t, h), BF16),
            vmem((2, t, h), BF16),
            vmem((2, 2, t, h), F32),
            dma((5,)),
            dma((2, 1)),
            dma((2, 3)),
            dma((2, 4)),
            dma((2, 2)),
            dma((2, 2)),
            dma((2, 2)),
            dma((2, 3)),
            dma((2, 3)),
            dma((2, 2)),
        ]
        outs = pl.pallas_call(
            make_kernel(n_ctx, n_tp, t),
            out_shape=(
                jax.ShapeDtypeStruct(queries.shape, BF16),
                jax.ShapeDtypeStruct(keys.shape, BF16),
                jax.ShapeDtypeStruct(values.shape, BF16),
            ),
            in_specs=[pl.BlockSpec(memory_space=pltpu.HBM)] * 5,
            out_specs=tuple(pl.BlockSpec(memory_space=pltpu.VMEM) for _ in range(3)),
            scratch_shapes=scratch,
            compiler_params=pltpu.CompilerParams(
                collective_id=0, has_side_effects=True, vmem_limit_bytes=48 << 20
            ),
            name="attention_backward",
        )(*(pltpu.with_memory_space_constraint(x, pltpu.HBM) for x in (layer_cotangent.T, out_weight.T, queries, keys, values)))
        return pl.pallas_call(
            write_out,
            out_shape=tuple(jax.ShapeDtypeStruct(o.shape, o.dtype) for o in outs),
            in_specs=[pl.BlockSpec(memory_space=pltpu.VMEM)] * 3,
            out_specs=tuple(pl.BlockSpec(memory_space=pl.ANY) for _ in outs),
            scratch_shapes=[dma((3,))],
            compiler_params=pltpu.CompilerParams(vmem_limit_bytes=4 << 20),
            name="write_out",
        )(*outs)

    in_specs = (P("ctx", "tp"), P(None, "tp"), P("ctx", "tp"), P("ctx", "tp"), P("ctx", "tp"))
    out_specs = (P("ctx", "tp"), P("ctx", "tp"), P("ctx", "tp"))
    return jax.shard_map(local, mesh=mesh, in_specs=in_specs, out_specs=out_specs, check_vma=False)
```

```python
import jax
import jax.numpy as jnp
from jax import lax
from jax.experimental import pallas as pl
from jax.experimental.pallas import tpu as pltpu
from jax.sharding import PartitionSpec as P

HEAD_SIZE = 128
Y = 4
score_scale = 168.0 ** (-0.5)
MESH = pl.DeviceIdType.MESH
F32 = jnp.float32
BF16 = jnp.bfloat16


def dot(a, b, ca, cb):
    return lax.dot_general(a, b, (((ca,), (cb,)), ((), ())), preferred_element_type=F32)


def write_out(dq_in, dk_in, dv_in, dq_out, dk_out, dv_out, sem):
    pairs = ((dq_in, dq_out), (dk_in, dk_out), (dv_in, dv_out))
    copies = [pltpu.make_async_copy(a, b, sem.at[i]) for i, (a, b) in enumerate(pairs)]
    for copy in copies:
        copy.start()
    for copy in copies:
        copy.wait()


def make_kernel(n_ctx, n_tp, t):
    n_u = n_tp // 2
    back = 4
    h = HEAD_SIZE
    order = (2, 1, 3, 0)

    def kernel(
        cot_hbm, w_hbm, q_hbm, k_hbm, v_hbm,
        dq_ref, dk_ref, dv_ref,
        cot_turned, cot, w, q_in, q2, kv, kt,
        pair_send, pair_recv, own_terms, own_part, ring_send, s1_recv, d_recv, c_recv, grads,
        probs, probs_low, dprobs, dscores,
        g_send, g_recv, z_send, z_recv, g_own,
        load_sem, kvz_sem, kvy_sem, pair_sem, s1_sem, d_sem, c_sem, gk_sem, gv_sem, z_sem, turn_sem,
    ):
        c = lax.axis_index("ctx")
        tp = lax.axis_index("tp")
        u = tp // 2
        a = tp % 2
        y = c % Y
        plane = c - y

        loads = [
            pltpu.make_async_copy(k_hbm, kv.at[back, 0], load_sem.at[0]),
            pltpu.make_async_copy(v_hbm, kv.at[back, 1], load_sem.at[1]),
            pltpu.make_async_copy(cot_hbm, cot_turned, load_sem.at[2]),
        ]
        for i, du in enumerate(order):
            columns = pl.ds(pl.multiple_of(((u + du) % n_u) * 4 * h, 4 * h), 4 * h)
            loads.append(pltpu.make_async_copy(w_hbm.at[:, columns], w.at[:, columns], load_sem.at[3 + i]))
        loads.append(pltpu.make_async_copy(q_hbm, q_in, load_sem.at[7]))
        loads[2].start()
        loads[3].start()

        following = ((c + back) % n_ctx, tp)
        preceding = ((c + n_ctx - back) % n_ctx, tp)
        other_core = (c, u * 2 + (1 - a))
        up = (c, (tp + 2) % n_tp)
        down = (c, (tp + n_tp - 2) % n_tp)

        def along(r):
            return (plane + (y + r) % Y, tp)

        barrier = pltpu.get_barrier_semaphore()
        partners = [following, preceding, other_core, up, down, along(1), along(2), along(3)]
        for partner in partners:
            pl.semaphore_signal(barrier, inc=1, device_id=partner, device_id_type=MESH)

        loads[0].start()
        loads[1].start()

        def remote(src, dst, sems, index, device):
            return pltpu.make_async_remote_copy(
                src_ref=src, dst_ref=dst, send_sem=sems.at[0, index], recv_sem=sems.at[1, index],
                device_id=device, device_id_type=MESH,
            )

        def part(du, core):
            dest = ((u + du) % n_u) * 2 + core
            columns = w[:, pl.ds(pl.multiple_of(dest * 2 * h, 2 * h), 2 * h)]
            return dot(cot[...], columns, 1, 0)

        pairs = []

        def for_other(i):
            loads[3 + i].wait()
            term = part(order[i], 1 - a)
            pair_send[i, 0:t] = term[:, :h].astype(BF16)
            pair_send[i, t:] = term[:, h:].astype(BF16)
            pairs.append(remote(pair_send.at[i], pair_recv.at[i], pair_sem, i, other_core))

        def for_this(i):
            own_terms[i] = part(order[i], a)

        def pair_sum(i):
            pairs[i].wait_recv()
            low = own_terms[i, :, :h] + pair_recv[i, 0:t].astype(F32)
            high = own_terms[i, :, h:] + pair_recv[i, t:].astype(F32)
            return low, high

        s1 = [
            remote(ring_send.at[0, 0], s1_recv.at[0], s1_sem, 0, up),
            remote(ring_send.at[0, 1], s1_recv.at[1], s1_sem, 1, down),
        ]
        direct = [
            remote(ring_send.at[1, 1], d_recv.at[0], d_sem, 0, up),
            remote(ring_send.at[2, 0], d_recv.at[1], d_sem, 1, down),
        ]
        combined = [
            remote(ring_send.at[1, 0], c_recv.at[0], c_sem, 0, up),
            remote(ring_send.at[2, 1], c_recv.at[1], c_sem, 1, down),
        ]
        loads[2].wait()
        cot[...] = cot_turned[...].T
        for load in loads[4:]:
            load.start()
        for_other(0)
        for_this(0)
        pl.semaphore_wait(barrier, len(partners))
        pairs[0].start()
        loads[0].wait()
        loads[1].wait()
        kvz = remote(kv.at[back], kv.at[0], kvz_sem, 0, following)
        kvz.start()
        for_other(1)
        for_other(2)
        low, high = pair_sum(0)
        ring_send[0, 0] = low.astype(BF16)
        ring_send[0, 1] = high.astype(BF16)

        @pl.when(a == 0)
        def _():
            s1[0].start()
            s1[1].start()

        pairs[1].start()
        pairs[2].start()
        for_other(3)
        pairs[3].start()
        for_this(1)
        for_this(2)
        for_this(3)
        low, high = pair_sum(1)
        ring_send[1, 1] = high.astype(BF16)
        own_part[0] = low
        low, high = pair_sum(2)
        ring_send[2, 0] = low.astype(BF16)
        own_part[1] = high
        low, high = pair_sum(3)
        own_part[2] = low
        own_part[3] = high

        @pl.when(a == 0)
        def _():
            s1[0].wait_send()
            s1[1].wait_send()
            pl.semaphore_signal(turn_sem, inc=1, device_id=other_core, device_id_type=MESH)
            direct[0].start()
            direct[1].start()

        kvz.wait_recv()
        kvy = []
        for r in (2, 1, 3):
            source = jnp.where(y < r, back, 0)
            copy = remote(kv.at[source], kv.at[r], kvy_sem, r - 1, along(Y - r))
            copy.start()
            kvy.append(copy)

        @pl.when(a == 1)
        def _():
            pl.semaphore_wait(turn_sem, 1)
            s1[0].start()
            s1[1].start()
            s1[0].wait_send()
            direct[0].start()
            s1[1].wait_send()
            direct[1].start()

        s1[0].wait_recv()
        ring_send[1, 0] = (own_part[0] + s1_recv[0].astype(F32)).astype(BF16)
        combined[0].start()
        s1[1].wait_recv()
        ring_send[2, 1] = (own_part[1] + s1_recv[1].astype(F32)).astype(BF16)
        combined[1].start()

        loads[7].wait()
        q2[0:t] = q_in[:, :h]
        q2[t:] = q_in[:, h:]

        key_row = lax.broadcasted_iota(jnp.int32, (t, 2 * t), 0)
        query_col = lax.broadcasted_iota(jnp.int32, (t, 2 * t), 1) % t
        top = jnp.full((1, 2 * t), -jnp.inf, F32)
        for slot in (4, 0, 2, 1, 3):
            if slot in (1, 2, 3):
                kvy[(2, 1, 3).index(slot)].wait_recv()
            scores = dot(kv[slot, 0], q2[...], 1, 1) * score_scale
            here = c + slot >= back
            if slot == back:
                scores = jnp.where(key_row <= query_col, scores, -jnp.inf)
            elif slot == 0:
                scores = jnp.where((key_row > query_col) & here, scores, -jnp.inf)
            else:
                scores = jnp.where(here, scores, -jnp.inf)
            probs[slot] = scores
            top = jnp.maximum(top, jnp.max(scores, axis=0, keepdims=True))
            kt[slot] = kv[slot, 0].T
        total = jnp.zeros((1, 2 * t), F32)
        for slot in range(back + 1):
            expo = jnp.exp(probs[slot] - top)
            probs[slot] = expo
            total = total + jnp.sum(expo, axis=0, keepdims=True)
        inverse = 1.0 / total
        for slot in range(back + 1):
            prob = probs[slot] * inverse
            probs[slot] = prob
            probs_low[slot] = prob.astype(BF16)

        direct[0].wait_recv()
        direct[1].wait_recv()
        combined[0].wait_recv()
        combined[1].wait_recv()
        grads[0:t] = (
            own_part[2] + d_recv[1].astype(F32) + c_recv[0].astype(F32)
        ).astype(BF16)
        grads[t:] = (
            own_part[3] + d_recv[0].astype(F32) + c_recv[1].astype(F32)
        ).astype(BF16)

        gk, gv = {}, {}
        for r in (1, 2, 3):
            gv[r] = remote(g_send.at[r - 1, 1], g_recv.at[r - 1, 1], gv_sem, r - 1, along(r))
            gk[r] = remote(g_send.at[r - 1, 0], g_recv.at[r - 1, 0], gk_sem, r - 1, along(r))
            g_send[r - 1, 1] = dot(probs_low[r], grads[...], 1, 0).astype(BF16)
            gv[r].start()
        delta = jnp.zeros((1, 2 * t), F32)
        for slot in range(back + 1):
            dp = dot(kv[slot, 1], grads[...], 1, 1)
            dprobs[slot] = dp
            delta = delta + jnp.sum(probs[slot] * dp, axis=0, keepdims=True)
        for slot in (1, 2, 3):
            ds = (probs[slot] * (dprobs[slot] - delta) * score_scale).astype(BF16)
            dscores[slot] = ds
            g_send[slot - 1, 0] = dot(ds, q2[...], 1, 0).astype(BF16)
            gk[slot].start()
        for slot in (0, 4):
            g_own[slot // 4, 1] = dot(probs_low[slot], grads[...], 1, 0)
        for slot in (0, 4):
            ds = (probs[slot] * (dprobs[slot] - delta) * score_scale).astype(BF16)
            dscores[slot] = ds
            g_own[slot // 4, 0] = dot(ds, q2[...], 1, 0)

        z_copies = [
            remote(z_send.at[i], z_recv.at[i], z_sem, i, preceding) for i in range(2)
        ]

        def add(i, copies, into):
            for r in (1, 2, 3):
                @pl.when((y >= r) if into == 0 else (y < r))
                def _():
                    copies[r].wait_recv()
                    g_own[into, i] += g_recv[r - 1, i].astype(F32)

        def pass_on(i, copies):
            add(i, copies, 0)
            z_send[i] = g_own[0, i].astype(BF16)
            z_copies[i].start()

        pass_on(1, gv)
        turned = jnp.zeros((h, 2 * t), F32)
        for slot in range(back + 1):
            turned = turned + dot(kt[slot], dscores[slot], 1, 0)
        dq_ref[:, :h] = turned[:, :t].T.astype(BF16)
        dq_ref[:, h:] = turned[:, t:].T.astype(BF16)
        pass_on(0, gk)
        add(1, gv, 1)
        add(0, gk, 1)
        z_copies[1].wait_recv()
        dv_ref[...] = (g_own[1, 1] + z_recv[1].astype(F32)).astype(BF16)
        z_copies[0].wait_recv()
        dk_ref[...] = (g_own[1, 0] + z_recv[0].astype(F32)).astype(BF16)

        for copy in [kvz, *kvy, *pairs, *combined, *gk.values(), *gv.values(), *z_copies]:
            copy.wait_send()

        direct[0].wait_send()
        direct[1].wait_send()

    return kernel


def solution(mesh):
    n_ctx, n_tp = mesh.shape["ctx"], mesh.shape["tp"]

    def local(layer_cotangent, out_weight, queries, keys, values):
        t, d = layer_cotangent.shape
        h = HEAD_SIZE
        vmem = pltpu.VMEM
        dma = pltpu.SemaphoreType.DMA
        scratch = [
            vmem((d, t), BF16),
            vmem((t, d), BF16),
            vmem(out_weight.shape[::-1], BF16),
            vmem((t, 2 * h), BF16),
            vmem((2 * t, h), BF16),
            vmem((5, 2, t, h), BF16),
            vmem((5, h, t), BF16),
            vmem((4, 2 * t, h), BF16),
            vmem((4, 2 * t, h), BF16),
            vmem((4, t, 2 * h), F32),
            vmem((4, t, h), F32),
            vmem((3, 2, t, h), BF16),
            vmem((2, t, h), BF16),
            vmem((2, t, h), BF16),
            vmem((2, t, h), BF16),
            vmem((2 * t, h), BF16),
            vmem((5, t, 2 * t), F32),
            vmem((5, t, 2 * t), BF16),
            vmem((5, t, 2 * t), F32),
            vmem((5, t, 2 * t), BF16),
            vmem((3, 2, t, h), BF16),
            vmem((3, 2, t, h), BF16),
            vmem((2, t, h), BF16),
            vmem((2, t, h), BF16),
            vmem((2, 2, t, h), F32),
            dma((8,)),
            dma((2, 1)),
            dma((2, 3)),
            dma((2, 4)),
            dma((2, 2)),
            dma((2, 2)),
            dma((2, 2)),
            dma((2, 3)),
            dma((2, 3)),
            dma((2, 2)),
            pltpu.SemaphoreType.REGULAR,
        ]
        outs = pl.pallas_call(
            make_kernel(n_ctx, n_tp, t),
            out_shape=(
                jax.ShapeDtypeStruct(queries.shape, BF16),
                jax.ShapeDtypeStruct(keys.shape, BF16),
                jax.ShapeDtypeStruct(values.shape, BF16),
            ),
            in_specs=[pl.BlockSpec(memory_space=pltpu.HBM)] * 5,
            out_specs=tuple(pl.BlockSpec(memory_space=pltpu.VMEM) for _ in range(3)),
            scratch_shapes=scratch,
            compiler_params=pltpu.CompilerParams(
                collective_id=0, has_side_effects=True, vmem_limit_bytes=48 << 20
            ),
            name="attention_backward",
        )(*(pltpu.with_memory_space_constraint(x, pltpu.HBM) for x in (layer_cotangent.T, out_weight.T, queries, keys, values)))
        return pl.pallas_call(
            write_out,
            out_shape=tuple(jax.ShapeDtypeStruct(o.shape, o.dtype) for o in outs),
            in_specs=[pl.BlockSpec(memory_space=pltpu.VMEM)] * 3,
            out_specs=tuple(pl.BlockSpec(memory_space=pl.ANY) for _ in outs),
            scratch_shapes=[dma((3,))],
            compiler_params=pltpu.CompilerParams(vmem_limit_bytes=4 << 20),
            name="write_out",
        )(*outs)

    in_specs = (P("ctx", "tp"), P(None, "tp"), P("ctx", "tp"), P("ctx", "tp"), P("ctx", "tp"))
    out_specs = (P("ctx", "tp"), P("ctx", "tp"), P("ctx", "tp"))
    return jax.shard_map(local, mesh=mesh, in_specs=in_specs, out_specs=out_specs, check_vma=False)
```

```python
import jax
import jax.numpy as jnp
from jax import lax
from jax.experimental import pallas as pl
from jax.experimental.pallas import tpu as pltpu
from jax.sharding import PartitionSpec as P

HEAD_SIZE = 128
Y = 4
score_scale = 168.0 ** (-0.5)
MESH = pl.DeviceIdType.MESH
F32 = jnp.float32
BF16 = jnp.bfloat16


def dot(a, b, ca, cb):
    return lax.dot_general(a, b, (((ca,), (cb,)), ((), ())), preferred_element_type=F32)


def write_out(dq_in, dk_in, dv_in, dq_out, dk_out, dv_out, sem):
    pairs = ((dq_in, dq_out), (dk_in, dk_out), (dv_in, dv_out))
    copies = [pltpu.make_async_copy(a, b, sem.at[i]) for i, (a, b) in enumerate(pairs)]
    for copy in copies:
        copy.start()
    for copy in copies:
        copy.wait()


def make_kernel(n_ctx, n_tp, t):
    n_u = n_tp // 2
    back = 4
    h = HEAD_SIZE
    order = (2, 1, 3, 0)

    def kernel(
        cot_hbm, w_hbm, q_hbm, k_hbm, v_hbm,
        dq_ref, dk_ref, dv_ref,
        cot_turned, cot, w, q_in, q2, kv, kt,
        pair_send, pair_recv, own_terms, own_part, ring_send, s1_recv, d_recv, c_recv, grads,
        probs, probs_low, dscores, vt, mixed_values, grads_turned,
        g_send, g_recv, z_send, z_recv, g_own,
        load_sem, kvz_sem, kvy_sem, pair_sem, s1_sem, d_sem, c_sem, gk_sem, gv_sem, z_sem, turn_sem,
    ):
        c = lax.axis_index("ctx")
        tp = lax.axis_index("tp")
        u = tp // 2
        a = tp % 2
        y = c % Y
        plane = c - y

        loads = [
            pltpu.make_async_copy(k_hbm, kv.at[back, 0], load_sem.at[0]),
            pltpu.make_async_copy(v_hbm, kv.at[back, 1], load_sem.at[1]),
            pltpu.make_async_copy(cot_hbm, cot_turned, load_sem.at[2]),
        ]
        for i, du in enumerate(order):
            columns = pl.ds(pl.multiple_of(((u + du) % n_u) * 4 * h, 4 * h), 4 * h)
            loads.append(pltpu.make_async_copy(w_hbm.at[:, columns], w.at[:, columns], load_sem.at[3 + i]))
        loads.append(pltpu.make_async_copy(q_hbm, q_in, load_sem.at[7]))
        following = ((c + back) % n_ctx, tp)
        preceding = ((c + n_ctx - back) % n_ctx, tp)
        other_core = (c, u * 2 + (1 - a))
        up = (c, (tp + 2) % n_tp)
        down = (c, (tp + n_tp - 2) % n_tp)

        def along(r):
            return (plane + (y + r) % Y, tp)

        barrier = pltpu.get_barrier_semaphore()
        partners = [up, down, following, preceding, along(2), along(1), along(3), other_core]
        for partner in partners:
            pl.semaphore_signal(barrier, inc=1, device_id=partner, device_id_type=MESH)

        for i in (2, 3, 0, 1):
            loads[i].start()

        def remote(src, dst, sems, index, device):
            return pltpu.make_async_remote_copy(
                src_ref=src, dst_ref=dst, send_sem=sems.at[0, index], recv_sem=sems.at[1, index],
                device_id=device, device_id_type=MESH,
            )

        def part(du, core):
            dest = ((u + du) % n_u) * 2 + core
            columns = w[:, pl.ds(pl.multiple_of(dest * 2 * h, 2 * h), 2 * h)]
            return dot(cot[...], columns, 1, 0)

        pairs = []

        def for_other(i):
            loads[3 + i].wait()
            term = part(order[i], 1 - a)
            pair_send[i, 0:t] = term[:, :h].astype(BF16)
            pair_send[i, t:] = term[:, h:].astype(BF16)
            pairs.append(remote(pair_send.at[i], pair_recv.at[i], pair_sem, i, other_core))

        def for_this(i):
            own_terms[i] = part(order[i], a)

        def pair_sum(i):
            pairs[i].wait_recv()
            low = own_terms[i, :, :h] + pair_recv[i, 0:t].astype(F32)
            high = own_terms[i, :, h:] + pair_recv[i, t:].astype(F32)
            return low, high

        s1 = [
            remote(ring_send.at[0, 0], s1_recv.at[0], s1_sem, 0, up),
            remote(ring_send.at[0, 1], s1_recv.at[1], s1_sem, 1, down),
        ]
        direct = [
            remote(ring_send.at[1, 1], d_recv.at[0], d_sem, 0, up),
            remote(ring_send.at[2, 0], d_recv.at[1], d_sem, 1, down),
        ]
        combined = [
            remote(ring_send.at[1, 0], c_recv.at[0], c_sem, 0, up),
            remote(ring_send.at[2, 1], c_recv.at[1], c_sem, 1, down),
        ]
        loads[2].wait()
        cot[...] = cot_turned[...].T
        for load in loads[4:]:
            load.start()
        for_other(0)
        for_this(0)
        pl.semaphore_wait(barrier, len(partners))
        pairs[0].start()
        loads[0].wait()
        loads[1].wait()
        kvz = remote(kv.at[back], kv.at[0], kvz_sem, 0, following)
        kvz.start()
        for_other(1)
        for_other(2)
        low, high = pair_sum(0)
        ring_send[0, 0] = low.astype(BF16)
        ring_send[0, 1] = high.astype(BF16)

        @pl.when(a == 0)
        def _():
            s1[0].start()
            s1[1].start()

        pairs[1].start()
        pairs[2].start()
        for_other(3)
        pairs[3].start()
        for_this(1)
        for_this(2)
        for_this(3)
        low, high = pair_sum(1)
        ring_send[1, 1] = high.astype(BF16)
        own_part[0] = low
        low, high = pair_sum(2)
        ring_send[2, 0] = low.astype(BF16)
        own_part[1] = high
        low, high = pair_sum(3)
        own_part[2] = low
        own_part[3] = high

        @pl.when(a == 0)
        def _():
            s1[0].wait_send()
            s1[1].wait_send()
            pl.semaphore_signal(turn_sem, inc=1, device_id=other_core, device_id_type=MESH)
            direct[0].start()
            direct[1].start()

        kvz.wait_recv()
        kvy = []
        for r in (2, 1, 3):
            source = jnp.where(y < r, back, 0)
            copy = remote(kv.at[source], kv.at[r], kvy_sem, r - 1, along(Y - r))
            copy.start()
            kvy.append(copy)

        @pl.when(a == 1)
        def _():
            pl.semaphore_wait(turn_sem, 1)
            s1[0].start()
            s1[1].start()
            s1[0].wait_send()
            direct[0].start()
            s1[1].wait_send()
            direct[1].start()

        s1[0].wait_recv()
        ring_send[1, 0] = (own_part[0] + s1_recv[0].astype(F32)).astype(BF16)
        combined[0].start()
        s1[1].wait_recv()
        ring_send[2, 1] = (own_part[1] + s1_recv[1].astype(F32)).astype(BF16)
        combined[1].start()

        loads[7].wait()
        q2[0:t] = q_in[:, :h]
        q2[t:] = q_in[:, h:]

        key_row = lax.broadcasted_iota(jnp.int32, (t, 2 * t), 0)
        query_col = lax.broadcasted_iota(jnp.int32, (t, 2 * t), 1) % t
        top = jnp.full((1, 2 * t), -jnp.inf, F32)
        for slot in (4, 0, 2, 1, 3):
            if slot in (1, 2, 3):
                kvy[(2, 1, 3).index(slot)].wait_recv()
            scores = dot(kv[slot, 0], q2[...], 1, 1) * score_scale
            here = c + slot >= back
            if slot == back:
                scores = jnp.where(key_row <= query_col, scores, -jnp.inf)
            elif slot == 0:
                scores = jnp.where((key_row > query_col) & here, scores, -jnp.inf)
            else:
                scores = jnp.where(here, scores, -jnp.inf)
            probs[slot] = scores
            top = jnp.maximum(top, jnp.max(scores, axis=0, keepdims=True))
            kt[slot] = kv[slot, 0].T
            vt[slot] = kv[slot, 1].T
        total = jnp.zeros((1, 2 * t), F32)
        for slot in range(back + 1):
            expo = jnp.exp(probs[slot] - top)
            probs[slot] = expo
            total = total + jnp.sum(expo, axis=0, keepdims=True)
        inverse = 1.0 / total
        mixed = jnp.zeros((h, 2 * t), F32)
        for slot in range(back + 1):
            prob = probs[slot] * inverse
            probs[slot] = prob * score_scale
            rough = prob.astype(BF16)
            probs_low[slot] = rough
            rest = (prob - rough.astype(F32)).astype(BF16)
            mixed = mixed + dot(vt[slot], rough, 1, 0) + dot(vt[slot], rest, 1, 0)
        mixed_values[...] = mixed

        direct[0].wait_recv()
        direct[1].wait_recv()
        combined[0].wait_recv()
        combined[1].wait_recv()
        low = (own_part[2] + d_recv[1].astype(F32) + c_recv[0].astype(F32)).astype(BF16)
        high = (own_part[3] + d_recv[0].astype(F32) + c_recv[1].astype(F32)).astype(BF16)
        grads[0:t] = low
        grads[t:] = high
        grads_turned[:, 0:t] = low.T
        grads_turned[:, t:] = high.T

        gk, gv = {}, {}
        for r in (1, 2, 3):
            gv[r] = remote(g_send.at[r - 1, 1], g_recv.at[r - 1, 1], gv_sem, r - 1, along(r))
            gk[r] = remote(g_send.at[r - 1, 0], g_recv.at[r - 1, 0], gk_sem, r - 1, along(r))
        value_parts = dot(probs_low[1:4].reshape(3 * t, 2 * t), grads[...], 1, 0)
        for r in (1, 2, 3):
            g_send[r - 1, 1] = value_parts[(r - 1) * t : r * t].astype(BF16)
            gv[r].start()
        delta = jnp.sum(mixed_values[...] * grads_turned[...].astype(F32), axis=0, keepdims=True)

        def score_grads(first, count):
            slots = slice(first, first + count)
            dp = dot(kv[slots, 1].reshape(count * t, h), grads_turned[...], 1, 0)
            ds = probs[slots].reshape(count * t, 2 * t) * (dp - delta)
            ds = ds.astype(BF16)
            dscores[slots] = ds.reshape(count, t, 2 * t)
            return ds

        key_parts = dot(score_grads(1, 3), q2[...], 1, 0)
        for slot in (1, 2, 3):
            g_send[slot - 1, 0] = key_parts[(slot - 1) * t : slot * t].astype(BF16)
            gk[slot].start()
        for slot in (0, 4):
            g_own[slot // 4, 1] = dot(probs_low[slot], grads[...], 1, 0)
            g_own[slot // 4, 0] = dot(score_grads(slot, 1), q2[...], 1, 0)

        z_copies = [
            remote(z_send.at[i], z_recv.at[i], z_sem, i, preceding) for i in range(2)
        ]

        def add(i, copies, into):
            for r in (1, 2, 3):
                @pl.when((y >= r) if into == 0 else (y < r))
                def _():
                    copies[r].wait_recv()
                    g_own[into, i] += g_recv[r - 1, i].astype(F32)

        def pass_on(i, copies):
            add(i, copies, 0)
            z_send[i] = g_own[0, i].astype(BF16)
            z_copies[i].start()

        pass_on(1, gv)
        turned = jnp.zeros((h, 2 * t), F32)
        for slot in range(back + 1):
            turned = turned + dot(kt[slot], dscores[slot], 1, 0)
        dq_ref[:, :h] = turned[:, :t].T.astype(BF16)
        dq_ref[:, h:] = turned[:, t:].T.astype(BF16)
        pass_on(0, gk)
        add(1, gv, 1)
        add(0, gk, 1)
        z_copies[1].wait_recv()
        dv_ref[...] = (g_own[1, 1] + z_recv[1].astype(F32)).astype(BF16)
        z_copies[0].wait_recv()
        dk_ref[...] = (g_own[1, 0] + z_recv[0].astype(F32)).astype(BF16)

        for copy in [kvz, *kvy, *pairs, *combined, *gk.values(), *gv.values(), *z_copies]:
            copy.wait_send()

        direct[0].wait_send()
        direct[1].wait_send()

    return kernel


def solution(mesh):
    n_ctx, n_tp = mesh.shape["ctx"], mesh.shape["tp"]

    def local(layer_cotangent, out_weight, queries, keys, values):
        t, d = layer_cotangent.shape
        h = HEAD_SIZE
        vmem = pltpu.VMEM
        dma = pltpu.SemaphoreType.DMA
        scratch = [
            vmem((d, t), BF16),
            vmem((t, d), BF16),
            vmem(out_weight.shape[::-1], BF16),
            vmem((t, 2 * h), BF16),
            vmem((2 * t, h), BF16),
            vmem((5, 2, t, h), BF16),
            vmem((5, h, t), BF16),
            vmem((4, 2 * t, h), BF16),
            vmem((4, 2 * t, h), BF16),
            vmem((4, t, 2 * h), F32),
            vmem((4, t, h), F32),
            vmem((3, 2, t, h), BF16),
            vmem((2, t, h), BF16),
            vmem((2, t, h), BF16),
            vmem((2, t, h), BF16),
            vmem((2 * t, h), BF16),
            vmem((5, t, 2 * t), F32),
            vmem((5, t, 2 * t), BF16),
            vmem((5, t, 2 * t), BF16),
            vmem((5, h, t), BF16),
            vmem((h, 2 * t), F32),
            vmem((h, 2 * t), BF16),
            vmem((3, 2, t, h), BF16),
            vmem((3, 2, t, h), BF16),
            vmem((2, t, h), BF16),
            vmem((2, t, h), BF16),
            vmem((2, 2, t, h), F32),
            dma((8,)),
            dma((2, 1)),
            dma((2, 3)),
            dma((2, 4)),
            dma((2, 2)),
            dma((2, 2)),
            dma((2, 2)),
            dma((2, 3)),
            dma((2, 3)),
            dma((2, 2)),
            pltpu.SemaphoreType.REGULAR,
        ]
        outs = pl.pallas_call(
            make_kernel(n_ctx, n_tp, t),
            out_shape=(
                jax.ShapeDtypeStruct(queries.shape, BF16),
                jax.ShapeDtypeStruct(keys.shape, BF16),
                jax.ShapeDtypeStruct(values.shape, BF16),
            ),
            in_specs=[pl.BlockSpec(memory_space=pltpu.HBM)] * 5,
            out_specs=tuple(pl.BlockSpec(memory_space=pltpu.VMEM) for _ in range(3)),
            scratch_shapes=scratch,
            compiler_params=pltpu.CompilerParams(
                collective_id=0, has_side_effects=True, vmem_limit_bytes=48 << 20
            ),
            name="attention_backward",
        )(*(pltpu.with_memory_space_constraint(x, pltpu.HBM) for x in (layer_cotangent.T, out_weight.T, queries, keys, values)))
        return pl.pallas_call(
            write_out,
            out_shape=tuple(jax.ShapeDtypeStruct(o.shape, o.dtype) for o in outs),
            in_specs=[pl.BlockSpec(memory_space=pltpu.VMEM)] * 3,
            out_specs=tuple(pl.BlockSpec(memory_space=pl.ANY) for _ in outs),
            scratch_shapes=[dma((3,))],
            compiler_params=pltpu.CompilerParams(vmem_limit_bytes=4 << 20),
            name="write_out",
        )(*outs)

    in_specs = (P("ctx", "tp"), P(None, "tp"), P("ctx", "tp"), P("ctx", "tp"), P("ctx", "tp"))
    out_specs = (P("ctx", "tp"), P("ctx", "tp"), P("ctx", "tp"))
    return jax.shard_map(local, mesh=mesh, in_specs=in_specs, out_specs=out_specs, check_vma=False)
```

```python
import jax
import jax.numpy as jnp
from jax import lax
from jax.experimental import pallas as pl
from jax.experimental.pallas import tpu as pltpu
from jax.sharding import PartitionSpec as P

HEAD_SIZE = 128
Y = 4
score_scale = 168.0 ** (-0.5)
MESH = pl.DeviceIdType.MESH
F32 = jnp.float32
BF16 = jnp.bfloat16


def dot(a, b, ca, cb):
    return lax.dot_general(a, b, (((ca,), (cb,)), ((), ())), preferred_element_type=F32)


def write_out(dq_in, dk_in, dv_in, dq_out, dk_out, dv_out, sem):
    pairs = ((dq_in, dq_out), (dk_in, dk_out), (dv_in, dv_out))
    copies = [pltpu.make_async_copy(a, b, sem.at[i]) for i, (a, b) in enumerate(pairs)]
    for copy in copies:
        copy.start()
    for copy in copies:
        copy.wait()


def make_kernel(n_ctx, n_tp, t):
    n_u = n_tp // 2
    back = 4
    h = HEAD_SIZE
    order = (2, 1, 3, 0)

    def kernel(
        cot_hbm, w_hbm, q_hbm, k_hbm, v_hbm,
        dq_ref, dk_ref, dv_ref,
        cot_turned, cot, w, q_in, q2, kv, kt,
        pair_send, pair_recv, own_terms, own_part, ring_send, s1_recv, d_recv, c_recv, grads,
        probs, probs_low, dscores, vt, mixed_values, grads_turned,
        g_send, g_recv, z_send, z_recv, g_own,
        load_sem, kvz_sem, kvy_sem, pair_sem, s1_sem, d_sem, c_sem, gk_sem, gv_sem, z_sem, turn_sem,
    ):
        c = lax.axis_index("ctx")
        tp = lax.axis_index("tp")
        u = tp // 2
        a = tp % 2
        y = c % Y
        plane = c - y
        early = (c // Y) % 4 == 1
        yields = ((c // Y) % 4 >= 2) & (a == 1)

        loads = [
            pltpu.make_async_copy(k_hbm, kv.at[back, 0], load_sem.at[0]),
            pltpu.make_async_copy(v_hbm, kv.at[back, 1], load_sem.at[1]),
            pltpu.make_async_copy(cot_hbm, cot_turned, load_sem.at[2]),
        ]
        for i, du in enumerate(order):
            columns = pl.ds(pl.multiple_of(((u + du) % n_u) * 4 * h, 4 * h), 4 * h)
            loads.append(pltpu.make_async_copy(w_hbm.at[:, columns], w.at[:, columns], load_sem.at[3 + i]))
        loads.append(pltpu.make_async_copy(q_hbm, q_in, load_sem.at[7]))
        following = ((c + back) % n_ctx, tp)
        preceding = ((c + n_ctx - back) % n_ctx, tp)
        other_core = (c, u * 2 + (1 - a))
        up = (c, (tp + 2) % n_tp)
        down = (c, (tp + n_tp - 2) % n_tp)

        def along(r):
            return (plane + (y + r) % Y, tp)

        barrier = pltpu.get_barrier_semaphore()
        partners = [up, down, following, preceding, along(2), along(1), along(3), other_core]
        for partner in partners:
            pl.semaphore_signal(barrier, inc=1, device_id=partner, device_id_type=MESH)

        for i in (2, 3, 0, 1):
            loads[i].start()

        def remote(src, dst, sems, index, device):
            return pltpu.make_async_remote_copy(
                src_ref=src, dst_ref=dst, send_sem=sems.at[0, index], recv_sem=sems.at[1, index],
                device_id=device, device_id_type=MESH,
            )

        def part(du, core):
            dest = ((u + du) % n_u) * 2 + core
            columns = w[:, pl.ds(pl.multiple_of(dest * 2 * h, 2 * h), 2 * h)]
            return dot(cot[...], columns, 1, 0)

        pairs = []

        def for_other(i):
            loads[3 + i].wait()
            term = part(order[i], 1 - a)
            pair_send[i, 0:t] = term[:, :h].astype(BF16)
            pair_send[i, t:] = term[:, h:].astype(BF16)
            pairs.append(remote(pair_send.at[i], pair_recv.at[i], pair_sem, i, other_core))

        def for_this(i):
            own_terms[i] = part(order[i], a)

        def pair_sum(i):
            pairs[i].wait_recv()
            low = own_terms[i, :, :h] + pair_recv[i, 0:t].astype(F32)
            high = own_terms[i, :, h:] + pair_recv[i, t:].astype(F32)
            return low, high

        s1 = [
            remote(ring_send.at[0, 0], s1_recv.at[0], s1_sem, 0, up),
            remote(ring_send.at[0, 1], s1_recv.at[1], s1_sem, 1, down),
        ]
        direct = [
            remote(ring_send.at[1, 1], d_recv.at[0], d_sem, 0, up),
            remote(ring_send.at[2, 0], d_recv.at[1], d_sem, 1, down),
        ]
        combined = [
            remote(ring_send.at[1, 0], c_recv.at[0], c_sem, 0, up),
            remote(ring_send.at[2, 1], c_recv.at[1], c_sem, 1, down),
        ]
        loads[2].wait()
        cot[...] = cot_turned[...].T
        for load in loads[4:]:
            load.start()
        for_other(0)
        for_this(0)
        pl.semaphore_wait(barrier, len(partners))
        pairs[0].start()
        loads[0].wait()
        loads[1].wait()
        kvz = remote(kv.at[back], kv.at[0], kvz_sem, 0, following)
        kvz.start()
        for_other(1)
        for_other(2)
        low, high = pair_sum(0)
        ring_send[0, 0] = low.astype(BF16)
        ring_send[0, 1] = high.astype(BF16)

        @pl.when(a == 0)
        def _():
            s1[0].start()
            s1[1].start()

        pairs[1].start()
        pairs[2].start()
        for_other(3)
        pairs[3].start()
        for_this(1)
        for_this(2)
        for_this(3)
        low, high = pair_sum(1)
        ring_send[1, 1] = high.astype(BF16)
        own_part[0] = low
        low, high = pair_sum(2)
        ring_send[2, 0] = low.astype(BF16)
        own_part[1] = high
        low, high = pair_sum(3)
        own_part[2] = low
        own_part[3] = high

        @pl.when(a == 0)
        def _():
            s1[0].wait_send()

            @pl.when(early)
            def _():
                pl.semaphore_signal(turn_sem, inc=1, device_id=other_core, device_id_type=MESH)

            s1[1].wait_send()

            @pl.when(jnp.logical_not(early))
            def _():
                pl.semaphore_signal(turn_sem, inc=1, device_id=other_core, device_id_type=MESH)

            direct[0].start()
            direct[1].start()

        kvz.wait_recv()
        kvy = []
        for r in (2, 1, 3):
            source = jnp.where(y < r, back, 0)
            copy = remote(kv.at[source], kv.at[r], kvy_sem, r - 1, along(Y - r))
            copy.start()
            kvy.append(copy)

        @pl.when(a == 1)
        def _():
            pl.semaphore_wait(turn_sem, 1)
            s1[0].start()
            s1[1].start()
            s1[0].wait_send()
            direct[0].start()
            s1[1].wait_send()

            @pl.when(jnp.logical_not(yields))
            def _():
                direct[1].start()


        s1[0].wait_recv()
        ring_send[1, 0] = (own_part[0] + s1_recv[0].astype(F32)).astype(BF16)
        combined[0].start()
        s1[1].wait_recv()
        ring_send[2, 1] = (own_part[1] + s1_recv[1].astype(F32)).astype(BF16)
        combined[1].start()

        @pl.when(yields)
        def _():
            direct[1].start()


        loads[7].wait()
        q2[0:t] = q_in[:, :h]
        q2[t:] = q_in[:, h:]

        key_row = lax.broadcasted_iota(jnp.int32, (t, 2 * t), 0)
        query_col = lax.broadcasted_iota(jnp.int32, (t, 2 * t), 1) % t
        top = jnp.full((1, 2 * t), -jnp.inf, F32)
        for slot in (4, 0, 2, 1, 3):
            if slot in (1, 2, 3):
                kvy[(2, 1, 3).index(slot)].wait_recv()
            scores = dot(kv[slot, 0], q2[...], 1, 1) * score_scale
            here = c + slot >= back
            if slot == back:
                scores = jnp.where(key_row <= query_col, scores, -jnp.inf)
            elif slot == 0:
                scores = jnp.where((key_row > query_col) & here, scores, -jnp.inf)
            else:
                scores = jnp.where(here, scores, -jnp.inf)
            probs[slot] = scores
            top = jnp.maximum(top, jnp.max(scores, axis=0, keepdims=True))
            kt[slot] = kv[slot, 0].T
            vt[slot] = kv[slot, 1].T
        total = jnp.zeros((1, 2 * t), F32)
        for slot in range(back + 1):
            expo = jnp.exp(probs[slot] - top)
            probs[slot] = expo
            total = total + jnp.sum(expo, axis=0, keepdims=True)
        inverse = 1.0 / total
        mixed = jnp.zeros((h, 2 * t), F32)
        for slot in range(back + 1):
            prob = probs[slot] * inverse
            probs[slot] = prob * score_scale
            rough = prob.astype(BF16)
            probs_low[slot] = rough
            rest = (prob - rough.astype(F32)).astype(BF16)
            mixed = mixed + dot(vt[slot], rough, 1, 0) + dot(vt[slot], rest, 1, 0)
        mixed_values[...] = mixed

        direct[0].wait_recv()
        direct[1].wait_recv()
        combined[0].wait_recv()
        combined[1].wait_recv()
        low = (own_part[2] + d_recv[1].astype(F32) + c_recv[0].astype(F32)).astype(BF16)
        high = (own_part[3] + d_recv[0].astype(F32) + c_recv[1].astype(F32)).astype(BF16)
        grads[0:t] = low
        grads[t:] = high
        grads_turned[:, 0:t] = low.T
        grads_turned[:, t:] = high.T

        gk, gv = {}, {}
        for r in (1, 2, 3):
            gv[r] = remote(g_send.at[r - 1, 1], g_recv.at[r - 1, 1], gv_sem, r - 1, along(r))
            gk[r] = remote(g_send.at[r - 1, 0], g_recv.at[r - 1, 0], gk_sem, r - 1, along(r))
        value_parts = dot(probs_low[1:4].reshape(3 * t, 2 * t), grads[...], 1, 0)
        for r in (1, 2, 3):
            g_send[r - 1, 1] = value_parts[(r - 1) * t : r * t].astype(BF16)
            gv[r].start()
        delta = jnp.sum(mixed_values[...] * grads_turned[...].astype(F32), axis=0, keepdims=True)

        def score_grads(first, count):
            slots = slice(first, first + count)
            dp = dot(kv[slots, 1].reshape(count * t, h), grads_turned[...], 1, 0)
            ds = probs[slots].reshape(count * t, 2 * t) * (dp - delta)
            ds = ds.astype(BF16)
            dscores[slots] = ds.reshape(count, t, 2 * t)
            return ds

        key_parts = dot(score_grads(1, 3), q2[...], 1, 0)
        for slot in (1, 2, 3):
            g_send[slot - 1, 0] = key_parts[(slot - 1) * t : slot * t].astype(BF16)
            gk[slot].start()
        for slot in (0, 4):
            g_own[slot // 4, 1] = dot(probs_low[slot], grads[...], 1, 0)
            g_own[slot // 4, 0] = dot(score_grads(slot, 1), q2[...], 1, 0)

        z_copies = [
            remote(z_send.at[i], z_recv.at[i], z_sem, i, preceding) for i in range(2)
        ]

        def add(i, copies, into):
            for r in (1, 2, 3):
                @pl.when((y >= r) if into == 0 else (y < r))
                def _():
                    copies[r].wait_recv()
                    g_own[into, i] += g_recv[r - 1, i].astype(F32)

        def pass_on(i, copies):
            add(i, copies, 0)
            z_send[i] = g_own[0, i].astype(BF16)
            z_copies[i].start()

        pass_on(1, gv)
        turned = jnp.zeros((h, 2 * t), F32)
        for slot in range(back + 1):
            turned = turned + dot(kt[slot], dscores[slot], 1, 0)
        dq_ref[:, :h] = turned[:, :t].T.astype(BF16)
        dq_ref[:, h:] = turned[:, t:].T.astype(BF16)
        pass_on(0, gk)
        add(1, gv, 1)
        add(0, gk, 1)
        z_copies[1].wait_recv()
        dv_ref[...] = (g_own[1, 1] + z_recv[1].astype(F32)).astype(BF16)
        z_copies[0].wait_recv()
        dk_ref[...] = (g_own[1, 0] + z_recv[0].astype(F32)).astype(BF16)

        for copy in [kvz, *kvy, *pairs, *combined, *gk.values(), *gv.values(), *z_copies]:
            copy.wait_send()

        direct[0].wait_send()
        direct[1].wait_send()

    return kernel


def solution(mesh):
    n_ctx, n_tp = mesh.shape["ctx"], mesh.shape["tp"]

    def local(layer_cotangent, out_weight, queries, keys, values):
        t, d = layer_cotangent.shape
        h = HEAD_SIZE
        vmem = pltpu.VMEM
        dma = pltpu.SemaphoreType.DMA
        scratch = [
            vmem((d, t), BF16),
            vmem((t, d), BF16),
            vmem(out_weight.shape[::-1], BF16),
            vmem((t, 2 * h), BF16),
            vmem((2 * t, h), BF16),
            vmem((5, 2, t, h), BF16),
            vmem((5, h, t), BF16),
            vmem((4, 2 * t, h), BF16),
            vmem((4, 2 * t, h), BF16),
            vmem((4, t, 2 * h), F32),
            vmem((4, t, h), F32),
            vmem((3, 2, t, h), BF16),
            vmem((2, t, h), BF16),
            vmem((2, t, h), BF16),
            vmem((2, t, h), BF16),
            vmem((2 * t, h), BF16),
            vmem((5, t, 2 * t), F32),
            vmem((5, t, 2 * t), BF16),
            vmem((5, t, 2 * t), BF16),
            vmem((5, h, t), BF16),
            vmem((h, 2 * t), F32),
            vmem((h, 2 * t), BF16),
            vmem((3, 2, t, h), BF16),
            vmem((3, 2, t, h), BF16),
            vmem((2, t, h), BF16),
            vmem((2, t, h), BF16),
            vmem((2, 2, t, h), F32),
            dma((8,)),
            dma((2, 1)),
            dma((2, 3)),
            dma((2, 4)),
            dma((2, 2)),
            dma((2, 2)),
            dma((2, 2)),
            dma((2, 3)),
            dma((2, 3)),
            dma((2, 2)),
            pltpu.SemaphoreType.REGULAR,
        ]
        outs = pl.pallas_call(
            make_kernel(n_ctx, n_tp, t),
            out_shape=(
                jax.ShapeDtypeStruct(queries.shape, BF16),
                jax.ShapeDtypeStruct(keys.shape, BF16),
                jax.ShapeDtypeStruct(values.shape, BF16),
            ),
            in_specs=[pl.BlockSpec(memory_space=pltpu.HBM)] * 5,
            out_specs=tuple(pl.BlockSpec(memory_space=pltpu.VMEM) for _ in range(3)),
            scratch_shapes=scratch,
            compiler_params=pltpu.CompilerParams(
                collective_id=0, has_side_effects=True, vmem_limit_bytes=48 << 20
            ),
            name="attention_backward",
        )(*(pltpu.with_memory_space_constraint(x, pltpu.HBM) for x in (layer_cotangent.T, out_weight.T, queries, keys, values)))
        return pl.pallas_call(
            write_out,
            out_shape=tuple(jax.ShapeDtypeStruct(o.shape, o.dtype) for o in outs),
            in_specs=[pl.BlockSpec(memory_space=pltpu.VMEM)] * 3,
            out_specs=tuple(pl.BlockSpec(memory_space=pl.ANY) for _ in outs),
            scratch_shapes=[dma((3,))],
            compiler_params=pltpu.CompilerParams(vmem_limit_bytes=4 << 20),
            name="write_out",
        )(*outs)

    in_specs = (P("ctx", "tp"), P(None, "tp"), P("ctx", "tp"), P("ctx", "tp"), P("ctx", "tp"))
    out_specs = (P("ctx", "tp"), P("ctx", "tp"), P("ctx", "tp"))
    return jax.shard_map(local, mesh=mesh, in_specs=in_specs, out_specs=out_specs, check_vma=False)
```

```python
import jax
import jax.numpy as jnp
from jax import lax
from jax.experimental import pallas as pl
from jax.experimental.pallas import tpu as pltpu
from jax.sharding import PartitionSpec as P

HEAD_SIZE = 128
Y = 4
score_scale = 168.0 ** (-0.5)
MESH = pl.DeviceIdType.MESH
F32 = jnp.float32
BF16 = jnp.bfloat16


def dot(a, b, ca, cb):
    return lax.dot_general(a, b, (((ca,), (cb,)), ((), ())), preferred_element_type=F32)


def write_out(dq_in, dk_in, dv_in, dq_out, dk_out, dv_out, sem):
    pairs = ((dq_in, dq_out), (dk_in, dk_out), (dv_in, dv_out))
    copies = [pltpu.make_async_copy(a, b, sem.at[i]) for i, (a, b) in enumerate(pairs)]
    for copy in copies:
        copy.start()
    for copy in copies:
        copy.wait()


def make_kernel(n_ctx, n_tp, t):
    n_u = n_tp // 2
    back = 4
    h = HEAD_SIZE
    order = (2, 1, 3, 0)

    def kernel(
        cot_hbm, w_hbm, q_hbm, k_hbm, v_hbm,
        dq_ref, dk_ref, dv_ref,
        cot_turned, cot, w, q_in, q2, kv, kt,
        pair_send, pair_recv, own_terms, own_part, ring_send, s1_recv, d_recv, c_recv, grads,
        probs, probs_low, dscores, vt, mixed_values, grads_turned,
        g_send, g_recv, z_send, z_recv, g_own,
        load_sem, kvz_sem, kvy_sem, pair_sem, s1_sem, d_sem, c_sem, gk_sem, gv_sem, z_sem, turn_sem,
    ):
        c = lax.axis_index("ctx")
        tp = lax.axis_index("tp")
        u = tp // 2
        a = tp % 2
        y = c % Y
        plane = c - y
        early = (c // Y) % 4 == 1
        yields = ((c // Y) % 4 == 3) & (a == 1)

        loads = [
            pltpu.make_async_copy(k_hbm, kv.at[back, 0], load_sem.at[0]),
            pltpu.make_async_copy(v_hbm, kv.at[back, 1], load_sem.at[1]),
            pltpu.make_async_copy(cot_hbm, cot_turned, load_sem.at[2]),
        ]
        for i, du in enumerate(order):
            columns = pl.ds(pl.multiple_of(((u + du) % n_u) * 4 * h, 4 * h), 4 * h)
            loads.append(pltpu.make_async_copy(w_hbm.at[:, columns], w.at[:, columns], load_sem.at[3 + i]))
        loads.append(pltpu.make_async_copy(q_hbm, q_in, load_sem.at[7]))
        following = ((c + back) % n_ctx, tp)
        preceding = ((c + n_ctx - back) % n_ctx, tp)
        other_core = (c, u * 2 + (1 - a))
        up = (c, (tp + 2) % n_tp)
        down = (c, (tp + n_tp - 2) % n_tp)

        def along(r):
            return (plane + (y + r) % Y, tp)

        barrier = pltpu.get_barrier_semaphore()
        partners = [up, down, following, preceding, along(2), along(1), along(3), other_core]
        for partner in partners:
            pl.semaphore_signal(barrier, inc=1, device_id=partner, device_id_type=MESH)

        for i in (2, 3, 0, 1):
            loads[i].start()

        def remote(src, dst, sems, index, device):
            return pltpu.make_async_remote_copy(
                src_ref=src, dst_ref=dst, send_sem=sems.at[0, index], recv_sem=sems.at[1, index],
                device_id=device, device_id_type=MESH,
            )

        def part(du, core):
            dest = ((u + du) % n_u) * 2 + core
            columns = w[:, pl.ds(pl.multiple_of(dest * 2 * h, 2 * h), 2 * h)]
            return dot(cot[...], columns, 1, 0)

        pairs = []

        def for_other(i):
            loads[3 + i].wait()
            term = part(order[i], 1 - a)
            pair_send[i, 0:t] = term[:, :h].astype(BF16)
            pair_send[i, t:] = term[:, h:].astype(BF16)
            pairs.append(remote(pair_send.at[i], pair_recv.at[i], pair_sem, i, other_core))

        def for_this(i):
            own_terms[i] = part(order[i], a)

        def pair_sum(i):
            pairs[i].wait_recv()
            low = own_terms[i, :, :h] + pair_recv[i, 0:t].astype(F32)
            high = own_terms[i, :, h:] + pair_recv[i, t:].astype(F32)
            return low, high

        s1 = [
            remote(ring_send.at[0, 0], s1_recv.at[0], s1_sem, 0, up),
            remote(ring_send.at[0, 1], s1_recv.at[1], s1_sem, 1, down),
        ]
        direct = [
            remote(ring_send.at[1, 1], d_recv.at[0], d_sem, 0, up),
            remote(ring_send.at[2, 0], d_recv.at[1], d_sem, 1, down),
        ]
        combined = [
            remote(ring_send.at[1, 0], c_recv.at[0], c_sem, 0, up),
            remote(ring_send.at[2, 1], c_recv.at[1], c_sem, 1, down),
        ]
        loads[2].wait()
        cot[...] = cot_turned[...].T
        for load in loads[4:]:
            load.start()
        for_other(0)
        for_this(0)
        pl.semaphore_wait(barrier, len(partners))
        pairs[0].start()
        loads[0].wait()
        loads[1].wait()
        kvz = remote(kv.at[back], kv.at[0], kvz_sem, 0, following)
        kvz.start()
        for_other(1)
        for_other(2)
        low, high = pair_sum(0)
        ring_send[0, 0] = low.astype(BF16)
        ring_send[0, 1] = high.astype(BF16)

        @pl.when(a == 0)
        def _():
            s1[0].start()
            s1[1].start()

        pairs[1].start()
        pairs[2].start()
        for_other(3)
        pairs[3].start()
        for_this(1)
        for_this(2)
        for_this(3)
        low, high = pair_sum(1)
        ring_send[1, 1] = high.astype(BF16)
        own_part[0] = low
        low, high = pair_sum(2)
        ring_send[2, 0] = low.astype(BF16)
        own_part[1] = high
        low, high = pair_sum(3)
        own_part[2] = low
        own_part[3] = high

        @pl.when(a == 0)
        def _():
            s1[0].wait_send()

            @pl.when(early)
            def _():
                pl.semaphore_signal(turn_sem, inc=1, device_id=other_core, device_id_type=MESH)

            s1[1].wait_send()

            @pl.when(jnp.logical_not(early))
            def _():
                pl.semaphore_signal(turn_sem, inc=1, device_id=other_core, device_id_type=MESH)

            direct[0].start()
            direct[1].start()

        kvz.wait_recv()
        kvy = []
        for r in (2, 1, 3):
            source = jnp.where(y < r, back, 0)
            copy = remote(kv.at[source], kv.at[r], kvy_sem, r - 1, along(Y - r))
            copy.start()
            kvy.append(copy)

        @pl.when(a == 1)
        def _():
            pl.semaphore_wait(turn_sem, 1)
            s1[0].start()
            s1[1].start()
            s1[0].wait_send()
            direct[0].start()
            s1[1].wait_send()

            @pl.when(jnp.logical_not(yields))
            def _():
                direct[1].start()


        s1[0].wait_recv()
        ring_send[1, 0] = (own_part[0] + s1_recv[0].astype(F32)).astype(BF16)
        combined[0].start()
        s1[1].wait_recv()
        ring_send[2, 1] = (own_part[1] + s1_recv[1].astype(F32)).astype(BF16)
        combined[1].start()

        @pl.when(yields)
        def _():
            direct[1].start()


        loads[7].wait()
        q2[0:t] = q_in[:, :h]
        q2[t:] = q_in[:, h:]

        key_row = lax.broadcasted_iota(jnp.int32, (t, 2 * t), 0)
        query_col = lax.broadcasted_iota(jnp.int32, (t, 2 * t), 1) % t
        top = jnp.full((1, 2 * t), -jnp.inf, F32)
        for slot in (4, 0, 2, 1, 3):
            if slot in (1, 2, 3):
                kvy[(2, 1, 3).index(slot)].wait_recv()
            scores = dot(kv[slot, 0], q2[...], 1, 1) * score_scale
            here = c + slot >= back
            if slot == back:
                scores = jnp.where(key_row <= query_col, scores, -jnp.inf)
            elif slot == 0:
                scores = jnp.where((key_row > query_col) & here, scores, -jnp.inf)
            else:
                scores = jnp.where(here, scores, -jnp.inf)
            probs[slot] = scores
            top = jnp.maximum(top, jnp.max(scores, axis=0, keepdims=True))
            kt[slot] = kv[slot, 0].T
            vt[slot] = kv[slot, 1].T
        total = jnp.zeros((1, 2 * t), F32)
        for slot in range(back + 1):
            expo = jnp.exp(probs[slot] - top)
            probs[slot] = expo
            total = total + jnp.sum(expo, axis=0, keepdims=True)
        inverse = 1.0 / total
        mixed = jnp.zeros((h, 2 * t), F32)
        for slot in range(back + 1):
            prob = probs[slot] * inverse
            probs[slot] = prob * score_scale
            rough = prob.astype(BF16)
            probs_low[slot] = rough
            rest = (prob - rough.astype(F32)).astype(BF16)
            mixed = mixed + dot(vt[slot], rough, 1, 0) + dot(vt[slot], rest, 1, 0)
        mixed_values[...] = mixed

        direct[0].wait_recv()
        direct[1].wait_recv()
        combined[0].wait_recv()
        combined[1].wait_recv()
        low = (own_part[2] + d_recv[1].astype(F32) + c_recv[0].astype(F32)).astype(BF16)
        high = (own_part[3] + d_recv[0].astype(F32) + c_recv[1].astype(F32)).astype(BF16)
        grads[0:t] = low
        grads[t:] = high
        grads_turned[:, 0:t] = low.T
        grads_turned[:, t:] = high.T

        gk, gv = {}, {}
        for r in (1, 2, 3):
            gv[r] = remote(g_send.at[r - 1, 1], g_recv.at[r - 1, 1], gv_sem, r - 1, along(r))
            gk[r] = remote(g_send.at[r - 1, 0], g_recv.at[r - 1, 0], gk_sem, r - 1, along(r))
        value_parts = dot(probs_low[1:4].reshape(3 * t, 2 * t), grads[...], 1, 0)
        for r in (1, 2, 3):
            g_send[r - 1, 1] = value_parts[(r - 1) * t : r * t].astype(BF16)
            gv[r].start()
        delta = jnp.sum(mixed_values[...] * grads_turned[...].astype(F32), axis=0, keepdims=True)

        def score_grads(first, count):
            slots = slice(first, first + count)
            dp = dot(kv[slots, 1].reshape(count * t, h), grads_turned[...], 1, 0)
            ds = probs[slots].reshape(count * t, 2 * t) * (dp - delta)
            ds = ds.astype(BF16)
            dscores[slots] = ds.reshape(count, t, 2 * t)
            return ds

        key_parts = dot(score_grads(1, 3), q2[...], 1, 0)
        for slot in (1, 2, 3):
            g_send[slot - 1, 0] = key_parts[(slot - 1) * t : slot * t].astype(BF16)
            gk[slot].start()
        for slot in (0, 4):
            g_own[slot // 4, 1] = dot(probs_low[slot], grads[...], 1, 0)
            g_own[slot // 4, 0] = dot(score_grads(slot, 1), q2[...], 1, 0)

        z_copies = [
            remote(z_send.at[i], z_recv.at[i], z_sem, i, preceding) for i in range(2)
        ]

        def add(i, copies, into):
            for r in (1, 2, 3):
                @pl.when((y >= r) if into == 0 else (y < r))
                def _():
                    copies[r].wait_recv()
                    g_own[into, i] += g_recv[r - 1, i].astype(F32)

        def pass_on(i, copies):
            add(i, copies, 0)
            z_send[i] = g_own[0, i].astype(BF16)
            z_copies[i].start()

        pass_on(1, gv)
        turned = jnp.zeros((h, 2 * t), F32)
        for slot in range(back + 1):
            turned = turned + dot(kt[slot], dscores[slot], 1, 0)
        dq_ref[:, :h] = turned[:, :t].T.astype(BF16)
        dq_ref[:, h:] = turned[:, t:].T.astype(BF16)
        pass_on(0, gk)
        add(1, gv, 1)
        add(0, gk, 1)
        z_copies[1].wait_recv()
        dv_ref[...] = (g_own[1, 1] + z_recv[1].astype(F32)).astype(BF16)
        z_copies[0].wait_recv()
        dk_ref[...] = (g_own[1, 0] + z_recv[0].astype(F32)).astype(BF16)

        for copy in [kvz, *kvy, *pairs, *combined, *gk.values(), *gv.values(), *z_copies]:
            copy.wait_send()

        direct[0].wait_send()
        direct[1].wait_send()

    return kernel


def solution(mesh):
    n_ctx, n_tp = mesh.shape["ctx"], mesh.shape["tp"]

    def local(layer_cotangent, out_weight, queries, keys, values):
        t, d = layer_cotangent.shape
        h = HEAD_SIZE
        vmem = pltpu.VMEM
        dma = pltpu.SemaphoreType.DMA
        scratch = [
            vmem((d, t), BF16),
            vmem((t, d), BF16),
            vmem(out_weight.shape[::-1], BF16),
            vmem((t, 2 * h), BF16),
            vmem((2 * t, h), BF16),
            vmem((5, 2, t, h), BF16),
            vmem((5, h, t), BF16),
            vmem((4, 2 * t, h), BF16),
            vmem((4, 2 * t, h), BF16),
            vmem((4, t, 2 * h), F32),
            vmem((4, t, h), F32),
            vmem((3, 2, t, h), BF16),
            vmem((2, t, h), BF16),
            vmem((2, t, h), BF16),
            vmem((2, t, h), BF16),
            vmem((2 * t, h), BF16),
            vmem((5, t, 2 * t), F32),
            vmem((5, t, 2 * t), BF16),
            vmem((5, t, 2 * t), BF16),
            vmem((5, h, t), BF16),
            vmem((h, 2 * t), F32),
            vmem((h, 2 * t), BF16),
            vmem((3, 2, t, h), BF16),
            vmem((3, 2, t, h), BF16),
            vmem((2, t, h), BF16),
            vmem((2, t, h), BF16),
            vmem((2, 2, t, h), F32),
            dma((8,)),
            dma((2, 1)),
            dma((2, 3)),
            dma((2, 4)),
            dma((2, 2)),
            dma((2, 2)),
            dma((2, 2)),
            dma((2, 3)),
            dma((2, 3)),
            dma((2, 2)),
            pltpu.SemaphoreType.REGULAR,
        ]
        outs = pl.pallas_call(
            make_kernel(n_ctx, n_tp, t),
            out_shape=(
                jax.ShapeDtypeStruct(queries.shape, BF16),
                jax.ShapeDtypeStruct(keys.shape, BF16),
                jax.ShapeDtypeStruct(values.shape, BF16),
            ),
            in_specs=[pl.BlockSpec(memory_space=pltpu.HBM)] * 5,
            out_specs=tuple(pl.BlockSpec(memory_space=pltpu.VMEM) for _ in range(3)),
            scratch_shapes=scratch,
            compiler_params=pltpu.CompilerParams(
                collective_id=0, has_side_effects=True, vmem_limit_bytes=48 << 20
            ),
            name="attention_backward",
        )(*(pltpu.with_memory_space_constraint(x, pltpu.HBM) for x in (layer_cotangent.T, out_weight.T, queries, keys, values)))
        return pl.pallas_call(
            write_out,
            out_shape=tuple(jax.ShapeDtypeStruct(o.shape, o.dtype) for o in outs),
            in_specs=[pl.BlockSpec(memory_space=pltpu.VMEM)] * 3,
            out_specs=tuple(pl.BlockSpec(memory_space=pl.ANY) for _ in outs),
            scratch_shapes=[dma((3,))],
            compiler_params=pltpu.CompilerParams(vmem_limit_bytes=4 << 20),
            name="write_out",
        )(*outs)

    in_specs = (P("ctx", "tp"), P(None, "tp"), P("ctx", "tp"), P("ctx", "tp"), P("ctx", "tp"))
    out_specs = (P("ctx", "tp"), P("ctx", "tp"), P("ctx", "tp"))
    return jax.shard_map(local, mesh=mesh, in_specs=in_specs, out_specs=out_specs, check_vma=False)
```

```python
import jax
import jax.numpy as jnp
from jax import lax
from jax.experimental import pallas as pl
from jax.experimental.pallas import tpu as pltpu
from jax.sharding import PartitionSpec as P

HEAD_SIZE = 128
Y = 4
score_scale = 168.0 ** (-0.5)
MESH = pl.DeviceIdType.MESH
F32 = jnp.float32
BF16 = jnp.bfloat16


def dot(a, b, ca, cb):
    return lax.dot_general(a, b, (((ca,), (cb,)), ((), ())), preferred_element_type=F32)


def write_out(dq_in, dk_in, dv_in, dq_out, dk_out, dv_out, sem):
    pairs = ((dq_in, dq_out), (dk_in, dk_out), (dv_in, dv_out))
    copies = [pltpu.make_async_copy(a, b, sem.at[i]) for i, (a, b) in enumerate(pairs)]
    for copy in copies:
        copy.start()
    for copy in copies:
        copy.wait()


def make_kernel(n_ctx, n_tp, t):
    n_u = n_tp // 2
    back = 4
    h = HEAD_SIZE
    order = (2, 1, 3, 0)

    def kernel(
        cot_hbm, w_hbm, q_hbm, k_hbm, v_hbm,
        dq_ref, dk_ref, dv_ref,
        cot_turned, cot, w, q_in, q2, kv, kt,
        pair_send, pair_recv, own_terms, own_part, ring_send, s1_recv, d_recv, c_recv, grads,
        probs, probs_low, dscores, vt, mixed_values, grads_turned,
        g_send, g_recv, z_send, z_recv, g_own,
        load_sem, kvz_sem, kvy_sem, pair_sem, s1_sem, d_sem, c_sem, gk_sem, gv_sem, z_sem, turn_sem,
    ):
        c = lax.axis_index("ctx")
        tp = lax.axis_index("tp")
        u = tp // 2
        a = tp % 2
        y = c % Y
        plane = c - y
        early = (c // Y) % 4 == 1
        yields = ((c // Y) % 4 >= 2) & (a == 1)

        loads = [
            pltpu.make_async_copy(k_hbm, kv.at[back, 0], load_sem.at[0]),
            pltpu.make_async_copy(v_hbm, kv.at[back, 1], load_sem.at[1]),
            pltpu.make_async_copy(cot_hbm, cot_turned, load_sem.at[2]),
        ]
        for i, du in enumerate(order):
            columns = pl.ds(pl.multiple_of(((u + du) % n_u) * 4 * h, 4 * h), 4 * h)
            loads.append(pltpu.make_async_copy(w_hbm.at[:, columns], w.at[:, columns], load_sem.at[3 + i]))
        loads.append(pltpu.make_async_copy(q_hbm, q_in, load_sem.at[7]))
        following = ((c + back) % n_ctx, tp)
        preceding = ((c + n_ctx - back) % n_ctx, tp)
        other_core = (c, u * 2 + (1 - a))
        up = (c, (tp + 2) % n_tp)
        down = (c, (tp + n_tp - 2) % n_tp)

        def along(r):
            return (plane + (y + r) % Y, tp)

        barrier = pltpu.get_barrier_semaphore()
        partners = [up, down, following, preceding, along(2), along(1), along(3), other_core]
        for partner in partners:
            pl.semaphore_signal(barrier, inc=1, device_id=partner, device_id_type=MESH)

        for i in (2, 3, 0, 1):
            loads[i].start()

        def remote(src, dst, sems, index, device):
            return pltpu.make_async_remote_copy(
                src_ref=src, dst_ref=dst, send_sem=sems.at[0, index], recv_sem=sems.at[1, index],
                device_id=device, device_id_type=MESH,
            )

        def part(du, core):
            dest = ((u + du) % n_u) * 2 + core
            columns = w[:, pl.ds(pl.multiple_of(dest * 2 * h, 2 * h), 2 * h)]
            return dot(cot[...], columns, 1, 0)

        pairs = []

        def for_other(i):
            loads[3 + i].wait()
            term = part(order[i], 1 - a)
            pair_send[i, 0:t] = term[:, :h].astype(BF16)
            pair_send[i, t:] = term[:, h:].astype(BF16)
            pairs.append(remote(pair_send.at[i], pair_recv.at[i], pair_sem, i, other_core))

        def for_this(i):
            own_terms[i] = part(order[i], a)

        def pair_sum(i):
            pairs[i].wait_recv()
            low = own_terms[i, :, :h] + pair_recv[i, 0:t].astype(F32)
            high = own_terms[i, :, h:] + pair_recv[i, t:].astype(F32)
            return low, high

        s1 = [
            remote(ring_send.at[0, 0], s1_recv.at[0], s1_sem, 0, up),
            remote(ring_send.at[0, 1], s1_recv.at[1], s1_sem, 1, down),
        ]
        direct = [
            remote(ring_send.at[1, 1], d_recv.at[0], d_sem, 0, up),
            remote(ring_send.at[2, 0], d_recv.at[1], d_sem, 1, down),
        ]
        combined = [
            remote(ring_send.at[1, 0], c_recv.at[0], c_sem, 0, up),
            remote(ring_send.at[2, 1], c_recv.at[1], c_sem, 1, down),
        ]
        loads[2].wait()
        cot[...] = cot_turned[...].T
        for load in loads[4:]:
            load.start()
        for_other(0)
        for_this(0)
        pl.semaphore_wait(barrier, len(partners))
        pairs[0].start()
        loads[0].wait()
        loads[1].wait()
        kvz = remote(kv.at[back], kv.at[0], kvz_sem, 0, following)
        kvz.start()
        for_other(1)
        for_other(2)
        low, high = pair_sum(0)
        ring_send[0, 0] = low.astype(BF16)
        ring_send[0, 1] = high.astype(BF16)

        @pl.when(a == 0)
        def _():
            s1[0].start()
            s1[1].start()

        pairs[1].start()
        pairs[2].start()
        for_other(3)
        pairs[3].start()
        for_this(1)
        for_this(2)
        for_this(3)
        low, high = pair_sum(1)
        ring_send[1, 1] = high.astype(BF16)
        own_part[0] = low
        low, high = pair_sum(2)
        ring_send[2, 0] = low.astype(BF16)
        own_part[1] = high
        low, high = pair_sum(3)
        own_part[2] = low
        own_part[3] = high

        @pl.when(a == 0)
        def _():
            s1[0].wait_send()

            @pl.when(early)
            def _():
                pl.semaphore_signal(turn_sem, inc=1, device_id=other_core, device_id_type=MESH)

            s1[1].wait_send()

            @pl.when(jnp.logical_not(early))
            def _():
                pl.semaphore_signal(turn_sem, inc=1, device_id=other_core, device_id_type=MESH)

            direct[0].start()
            direct[1].start()

        kvz.wait_recv()
        kvy = []
        for r in (2, 1, 3):
            source = jnp.where(y < r, back, 0)
            copy = remote(kv.at[source], kv.at[r], kvy_sem, r - 1, along(Y - r))
            copy.start()
            kvy.append(copy)

        @pl.when(a == 1)
        def _():
            pl.semaphore_wait(turn_sem, 1)
            s1[0].start()
            s1[1].start()
            s1[0].wait_send()
            direct[0].start()
            s1[1].wait_send()

            @pl.when(jnp.logical_not(yields))
            def _():
                direct[1].start()


        s1[0].wait_recv()
        ring_send[1, 0] = (own_part[0] + s1_recv[0].astype(F32)).astype(BF16)
        combined[0].start()
        s1[1].wait_recv()
        ring_send[2, 1] = (own_part[1] + s1_recv[1].astype(F32)).astype(BF16)
        combined[1].start()

        @pl.when(yields)
        def _():
            direct[1].start()


        loads[7].wait()
        q2[0:t] = q_in[:, :h]
        q2[t:] = q_in[:, h:]

        key_row = lax.broadcasted_iota(jnp.int32, (t, 2 * t), 0)
        query_col = lax.broadcasted_iota(jnp.int32, (t, 2 * t), 1) % t
        top = jnp.full((1, 2 * t), -jnp.inf, F32)
        for slot in (4, 0, 2, 1, 3):
            if slot in (1, 2, 3):
                kvy[(2, 1, 3).index(slot)].wait_recv()
            scores = dot(kv[slot, 0], q2[...], 1, 1) * score_scale
            here = c + slot >= back
            if slot == back:
                scores = jnp.where(key_row <= query_col, scores, -jnp.inf)
            elif slot == 0:
                scores = jnp.where((key_row > query_col) & here, scores, -jnp.inf)
            else:
                scores = jnp.where(here, scores, -jnp.inf)
            probs[slot] = scores
            top = jnp.maximum(top, jnp.max(scores, axis=0, keepdims=True))
            kt[slot] = kv[slot, 0].T
            vt[slot] = kv[slot, 1].T
        total = jnp.zeros((1, 2 * t), F32)
        for slot in range(back + 1):
            expo = jnp.exp(probs[slot] - top)
            probs[slot] = expo
            total = total + jnp.sum(expo, axis=0, keepdims=True)
        inverse = 1.0 / total
        mixed = jnp.zeros((h, 2 * t), F32)
        for slot in range(back + 1):
            prob = probs[slot] * inverse
            probs[slot] = prob * score_scale
            rough = prob.astype(BF16)
            probs_low[slot] = rough
            rest = (prob - rough.astype(F32)).astype(BF16)
            mixed = mixed + dot(vt[slot], rough, 1, 0) + dot(vt[slot], rest, 1, 0)
        mixed_values[...] = mixed

        direct[0].wait_recv()
        direct[1].wait_recv()
        combined[0].wait_recv()
        combined[1].wait_recv()
        low = (own_part[2] + d_recv[1].astype(F32) + c_recv[0].astype(F32)).astype(BF16)
        high = (own_part[3] + d_recv[0].astype(F32) + c_recv[1].astype(F32)).astype(BF16)
        grads[0:t] = low
        grads[t:] = high
        grads_turned[:, 0:t] = low.T
        grads_turned[:, t:] = high.T

        gk, gv = {}, {}
        for r in (1, 2, 3):
            gv[r] = remote(g_send.at[r - 1, 1], g_recv.at[r - 1, 1], gv_sem, r - 1, along(r))
            gk[r] = remote(g_send.at[r - 1, 0], g_recv.at[r - 1, 0], gk_sem, r - 1, along(r))
        value_parts = dot(probs_low[1:4].reshape(3 * t, 2 * t), grads[...], 1, 0)
        for r in (1, 2, 3):
            g_send[r - 1, 1] = value_parts[(r - 1) * t : r * t].astype(BF16)
            gv[r].start()
        delta = jnp.sum(mixed_values[...] * grads_turned[...].astype(F32), axis=0, keepdims=True)

        def score_grads(first, count):
            slots = slice(first, first + count)
            dp = dot(kv[slots, 1].reshape(count * t, h), grads_turned[...], 1, 0)
            ds = probs[slots].reshape(count * t, 2 * t) * (dp - delta)
            ds = ds.astype(BF16)
            dscores[slots] = ds.reshape(count, t, 2 * t)
            return ds

        key_parts = dot(score_grads(1, 3), q2[...], 1, 0)
        for slot in (1, 2, 3):
            g_send[slot - 1, 0] = key_parts[(slot - 1) * t : slot * t].astype(BF16)
            gk[slot].start()

        def kept(slot):
            g_own[slot // 4, 1] = dot(probs_low[slot], grads[...], 1, 0)
            g_own[slot // 4, 0] = dot(score_grads(slot, 1), q2[...], 1, 0)

        kept(0)

        z_copies = [
            remote(z_send.at[i], z_recv.at[i], z_sem, i, preceding) for i in range(2)
        ]

        def add(i, copies, into):
            for r in (1, 2, 3):
                @pl.when((y >= r) if into == 0 else (y < r))
                def _():
                    copies[r].wait_recv()
                    g_own[into, i] += g_recv[r - 1, i].astype(F32)

        def pass_on(i, copies):
            add(i, copies, 0)
            z_send[i] = g_own[0, i].astype(BF16)
            z_copies[i].start()

        pass_on(1, gv)
        kept(4)
        pass_on(0, gk)
        turned = jnp.zeros((h, 2 * t), F32)
        for slot in range(back + 1):
            turned = turned + dot(kt[slot], dscores[slot], 1, 0)
        dq_ref[:, :h] = turned[:, :t].T.astype(BF16)
        dq_ref[:, h:] = turned[:, t:].T.astype(BF16)
        add(1, gv, 1)
        add(0, gk, 1)
        z_copies[1].wait_recv()
        dv_ref[...] = (g_own[1, 1] + z_recv[1].astype(F32)).astype(BF16)
        z_copies[0].wait_recv()
        dk_ref[...] = (g_own[1, 0] + z_recv[0].astype(F32)).astype(BF16)

        for copy in [kvz, *kvy, *pairs, *combined, *gk.values(), *gv.values(), *z_copies]:
            copy.wait_send()

        direct[0].wait_send()
        direct[1].wait_send()

    return kernel


def solution(mesh):
    n_ctx, n_tp = mesh.shape["ctx"], mesh.shape["tp"]

    def local(layer_cotangent, out_weight, queries, keys, values):
        t, d = layer_cotangent.shape
        h = HEAD_SIZE
        vmem = pltpu.VMEM
        dma = pltpu.SemaphoreType.DMA
        scratch = [
            vmem((d, t), BF16),
            vmem((t, d), BF16),
            vmem(out_weight.shape[::-1], BF16),
            vmem((t, 2 * h), BF16),
            vmem((2 * t, h), BF16),
            vmem((5, 2, t, h), BF16),
            vmem((5, h, t), BF16),
            vmem((4, 2 * t, h), BF16),
            vmem((4, 2 * t, h), BF16),
            vmem((4, t, 2 * h), F32),
            vmem((4, t, h), F32),
            vmem((3, 2, t, h), BF16),
            vmem((2, t, h), BF16),
            vmem((2, t, h), BF16),
            vmem((2, t, h), BF16),
            vmem((2 * t, h), BF16),
            vmem((5, t, 2 * t), F32),
            vmem((5, t, 2 * t), BF16),
            vmem((5, t, 2 * t), BF16),
            vmem((5, h, t), BF16),
            vmem((h, 2 * t), F32),
            vmem((h, 2 * t), BF16),
            vmem((3, 2, t, h), BF16),
            vmem((3, 2, t, h), BF16),
            vmem((2, t, h), BF16),
            vmem((2, t, h), BF16),
            vmem((2, 2, t, h), F32),
            dma((8,)),
            dma((2, 1)),
            dma((2, 3)),
            dma((2, 4)),
            dma((2, 2)),
            dma((2, 2)),
            dma((2, 2)),
            dma((2, 3)),
            dma((2, 3)),
            dma((2, 2)),
            pltpu.SemaphoreType.REGULAR,
        ]
        outs = pl.pallas_call(
            make_kernel(n_ctx, n_tp, t),
            out_shape=(
                jax.ShapeDtypeStruct(queries.shape, BF16),
                jax.ShapeDtypeStruct(keys.shape, BF16),
                jax.ShapeDtypeStruct(values.shape, BF16),
            ),
            in_specs=[pl.BlockSpec(memory_space=pltpu.HBM)] * 5,
            out_specs=tuple(pl.BlockSpec(memory_space=pltpu.VMEM) for _ in range(3)),
            scratch_shapes=scratch,
            compiler_params=pltpu.CompilerParams(
                collective_id=0, has_side_effects=True, vmem_limit_bytes=48 << 20
            ),
            name="attention_backward",
        )(*(pltpu.with_memory_space_constraint(x, pltpu.HBM) for x in (layer_cotangent.T, out_weight.T, queries, keys, values)))
        return pl.pallas_call(
            write_out,
            out_shape=tuple(jax.ShapeDtypeStruct(o.shape, o.dtype) for o in outs),
            in_specs=[pl.BlockSpec(memory_space=pltpu.VMEM)] * 3,
            out_specs=tuple(pl.BlockSpec(memory_space=pl.ANY) for _ in outs),
            scratch_shapes=[dma((3,))],
            compiler_params=pltpu.CompilerParams(vmem_limit_bytes=4 << 20),
            name="write_out",
        )(*outs)

    in_specs = (P("ctx", "tp"), P(None, "tp"), P("ctx", "tp"), P("ctx", "tp"), P("ctx", "tp"))
    out_specs = (P("ctx", "tp"), P("ctx", "tp"), P("ctx", "tp"))
    return jax.shard_map(local, mesh=mesh, in_specs=in_specs, out_specs=out_specs, check_vma=False)
```
